256 devices in a mesh: freq: 4 (over y_hi, core), slab: 64 (over y_lo, z, x).
Axes of the slice: x: 4, y: 4 (y_hi: 2, y_lo: 2; y = y_hi * 2 + y_lo), z: 8, core: 2. Of those that a mesh axis runs over, the one named last changes fastest.
Arguments:
- inverse_permittivity: float32 [512, 24, 512], P('slab'), may hold values from 0.083 to 1
- forward_fields: float32 [4, 6, 512, 24, 512], P('freq', None, 'slab'), may hold values from -6 to 6
- adjoint_fields: float32 [4, 6, 512, 24, 512], P('freq', None, 'slab'), may hold values from -6 to 6
- source_wave: float32 [4, 3], P('freq'), may hold values from -4 to 4
- source_profile: float32 [4, 512], P('freq'), may hold values from -4 to 4
- adjoint_wave: float32 [4, 3], P('freq'), may hold values from -4 to 4
- adjoint_profile: float32 [4, 512], P('freq'), may hold values from -4 to 4
- source_plane: int32 [4], P('freq'), may hold values from 0 to 23
- monitor_plane: int32 [4], P('freq'), may hold values from 0 to 23
- radius_map: int32 [64, 8], P('slab'), may hold values from 1 to 4
- design_mask: int32 [64, 8], P('slab'), may hold values 0 or 1
- design_density: float32 [512, 512], P('slab'), may hold values from 0 to 1
Outputs:
- forward_out: float32 [4, 6, 512, 24, 512], P('freq', None, 'slab')
- adjoint_out: float32 [4, 6, 512, 24, 512], P('freq', None, 'slab')
- projected: float32 [512, 512], P('slab')
The draws below stay inside these ranges and needn't reach their ends.
Inputs may be any that keep to these rules, and one draw needn't show every extreme that they name: `radius_map`: filter radius of a tile in cells.
All inputs are finite; a program needn't handle non-finite values. No bound on the sum of `design_mask` on one device may be relied on, other than what follows from the above.
Results may differ from the reference program's by a relative error of at most 0.0003.
Values sent between devices are 32-bit elements; how exact they have to be, the bound alone decides.
A program may use at most 64 MiB of HBM per device.

```python
import math
import jax
import jax.numpy as jnp
from jax import lax

NY = 512
NZ = 24
FREQS = 4
STEPS = 3
RMAX = 4
XTILES = 8
NX = 512
YTILES = 64
TILE_Y = 8
TILE_X = 64


def with_ends(drawn, key, smallest, top_value):
    dims = drawn.shape
    place = [jax.random.randint(jax.random.fold_in(key, axis), (), 0, dims[axis]) for axis in range(len(dims))]
    drawn = drawn.at[tuple(place)].set(smallest)
    longest = dims.index(max(dims))
    place[longest] = (place[longest] + 1) % dims[longest]
    return drawn.at[tuple(place)].set(top_value)


def steps_of(key, shape, shards, least, top_value):
    gain, own = 1.0, jax.random.fold_in(key, 6)
    for axis_at, shards_of in shards:
        heights = jnp.exp(jax.random.uniform(jax.random.fold_in(own, axis_at), (shards_of,), jnp.float32, least / len(shards), top_value / len(shards)))
        gain = gain * jnp.repeat(heights, shape[axis_at] // shards_of).reshape([-1 if axis == axis_at else 1 for axis in range(len(shape))])
    return gain


def bell_draw(key, shape, spread, bound, pieces=(), kind=jnp.bfloat16):
    array = jax.random.normal(key, shape, jnp.float32) * spread
    if len(pieces) > 0:
        array = steps_of(key, shape, pieces, -0.22, 0.18) * array
    return jnp.clip(array, min=-bound, max=bound).astype(kind)


def setup_inputs(seed: int = 0) -> dict:
    keys = jax.random.split(jax.random.key(seed), 13)
    inverse_permittivity = jnp.clip(jnp.exp(math.log(1.0) - 2.4889147 * jax.random.uniform(keys[0], (NX, NZ, NY), jnp.float32) ** steps_of(keys[0], (NX, NZ, NY), ((0, 64),), -0.2, 0.2)), 0.083, 1.0)
    forward_fields = bell_draw(keys[1], (FREQS, 6, NX, NZ, NY), 1.0, 6.0, ((0, 4), (2, 64)), jnp.float32)
    adjoint_fields = bell_draw(keys[2], (FREQS, 6, NX, NZ, NY), 1.0, 6.0, ((0, 4), (2, 64)), jnp.float32)
    source_wave = bell_draw(keys[3], (FREQS, STEPS), 1.0, 4.0, ((0, 4),), jnp.float32)
    source_profile = bell_draw(keys[4], (FREQS, NY), 1.0, 4.0, ((0, 4),), jnp.float32)
    adjoint_wave = bell_draw(keys[5], (FREQS, STEPS), 1.0, 4.0, ((0, 4),), jnp.float32)
    adjoint_profile = bell_draw(keys[6], (FREQS, NY), 1.0, 4.0, ((0, 4),), jnp.float32)
    source_plane = with_ends(jax.random.randint(keys[7], (FREQS,), 0, NZ), jax.random.fold_in(keys[7], 1), 0, NZ - 1).astype(jnp.int32)
    monitor_plane = with_ends(jax.random.randint(keys[8], (FREQS,), 0, NZ), jax.random.fold_in(keys[8], 1), 0, NZ - 1).astype(jnp.int32)
    radius_map = with_ends(jax.random.randint(keys[9], (YTILES, XTILES), 1, RMAX + 1), jax.random.fold_in(keys[9], 1), 1, RMAX).astype(jnp.int32)
    design_mask = with_ends((jax.random.randint(keys[10], (YTILES, XTILES), 0, 4) < 3).astype(jnp.int32), jax.random.fold_in(keys[10], 1), 0, 1)
    design_density = jnp.clip(1.0 * jax.random.uniform(keys[11], (NY, NX), jnp.float32) ** steps_of(keys[11], (NY, NX), ((0, 64),), -0.2, 0.2), 0.0, 1.0)
    return dict(inverse_permittivity=inverse_permittivity, forward_fields=forward_fields, adjoint_fields=adjoint_fields, source_wave=source_wave, source_profile=source_profile, adjoint_wave=adjoint_wave, adjoint_profile=adjoint_profile, source_plane=source_plane, monitor_plane=monitor_plane, radius_map=radius_map, design_mask=design_mask, design_density=design_density)


courant = 0.5
sharpness = 4.0
midpoint = 0.5
step_size = 0.3

def forward_cell(field, axis):
    axis = field.ndim + axis
    size = field.shape[axis]
    inner = lax.slice_in_dim(field, 1, size, axis=axis)
    edge = jnp.zeros_like(lax.slice_in_dim(field, 0, 1, axis=axis))
    return jnp.concatenate([inner, edge], axis=axis)

def backward_cell(field, axis):
    axis = field.ndim + axis
    size = field.shape[axis]
    inner = lax.slice_in_dim(field, 0, size - 1, axis=axis)
    edge = jnp.zeros_like(lax.slice_in_dim(field, 0, 1, axis=axis))
    return jnp.concatenate([edge, inner], axis=axis)

def yee_update(fields, inverse, source):
    elec_x, elec_y, elec_z, magn_x, magn_y, magn_z = fields
    magn_x = magn_x - courant * (forward_cell(elec_z, -1) - elec_z - (forward_cell(elec_y, -2) - elec_y))
    magn_y = magn_y - courant * (forward_cell(elec_x, -2) - elec_x - (forward_cell(elec_z, -3) - elec_z))
    magn_z = magn_z - courant * (forward_cell(elec_y, -3) - elec_y - (forward_cell(elec_x, -1) - elec_x))
    elec_x = elec_x + courant * inverse * (magn_z - backward_cell(magn_z, -1) - (magn_y - backward_cell(magn_y, -2))) + source
    elec_y = elec_y + courant * inverse * (magn_x - backward_cell(magn_x, -2) - (magn_z - backward_cell(magn_z, -3)))
    elec_z = elec_z + courant * inverse * (magn_y - backward_cell(magn_y, -3) - (magn_x - backward_cell(magn_x, -1)))
    return (elec_x, elec_y, elec_z, magn_x, magn_y, magn_z)

def reference(inverse_permittivity, forward_fields, adjoint_fields, source_wave, source_profile, adjoint_wave, adjoint_profile, source_plane, monitor_plane, radius_map, design_mask, design_density):
    waves = jnp.stack([source_wave, adjoint_wave], axis=1)
    profiles = jnp.stack([source_profile, adjoint_profile], axis=1)
    planes = jnp.stack([source_plane, monitor_plane], axis=1)

    def run_group(inputs):
        forward, adjoint, wave, profile, plane = inputs
        fields = tuple((jnp.stack([forward[component], adjoint[component]]) for component in range(6)))
        plane_hit = (jnp.arange(NZ, dtype=jnp.int32)[None, :] == plane[:, None]).astype(jnp.float32)
        intersection = jnp.zeros((NX, NY), jnp.float32)
        for turn in range(STEPS):
            source = wave[:, turn][:, None, None, None] * plane_hit[:, None, :, None] * profile[:, None, None, :]
            fields = yee_update(fields, inverse_permittivity, source)
            total = 0.0
            for component in range(3):
                total = total + fields[component][0] * fields[component][1]
            intersection = intersection + lax.optimization_barrier(jnp.sum(total, axis=1))
        return (jnp.stack([member[0] for member in fields]), jnp.stack([member[1] for member in fields]), intersection)
    forward_out, adjoint_out, intersections = lax.map(run_group, (forward_fields, adjoint_fields, waves, profiles, planes))
    gradient = lax.optimization_barrier(jnp.sum(intersections, axis=0))
    radius = jnp.repeat(jnp.repeat(radius_map, TILE_Y, axis=0), TILE_X, axis=1).astype(jnp.float32)
    chosen = jnp.repeat(jnp.repeat(design_mask, TILE_Y, axis=0), TILE_X, axis=1).astype(jnp.float32)
    scale = step_size / math.sqrt(3 * STEPS * NZ * FREQS)
    updated = design_density + scale * chosen * gradient.T
    padded = jnp.pad(updated, RMAX)
    inside = jnp.pad(jnp.ones((NY, NX), jnp.float32), RMAX)
    numerator = jnp.zeros((NY, NX), jnp.float32)
    weight_total = jnp.zeros((NY, NX), jnp.float32)
    for offset_y in range(2 * RMAX + 1):
        for offset_x in range(2 * RMAX + 1):
            distance = jnp.sqrt(jnp.asarray((offset_y - RMAX) ** 2 + (offset_x - RMAX) ** 2, jnp.float32))
            weight = jnp.maximum(radius - distance, 0.0)
            piece = padded[offset_y:offset_y + NY, offset_x:offset_x + NX]
            present = inside[offset_y:offset_y + NY, offset_x:offset_x + NX]
            numerator = numerator + weight * present * piece
            weight_total = weight_total + weight * present
    filtered = numerator / weight_total
    base = math.tanh(sharpness * midpoint)
    projected = (base + jnp.tanh(sharpness * (filtered - midpoint))) / (base + math.tanh(sharpness * (1.0 - midpoint)))
    return (forward_out, adjoint_out, projected)
```

```python
import math

import jax
import jax.numpy as jnp
from jax import lax
from jax.experimental import pallas as pl
from jax.experimental.pallas import tpu as pltpu
from jax.sharding import PartitionSpec as P

NY = 512
NZ = 24
FREQS = 4
STEPS = 3
RMAX = 4


courant = 0.5
sharpness = 4.0
midpoint = 0.5
step_size = 0.3


def next_y(v):
    lane = lax.broadcasted_iota(jnp.int32, v.shape, 1)
    return jnp.where(lane == v.shape[1] - 1, 0.0, pltpu.roll(v, v.shape[1] - 1, 1))


def prior_y(v):
    lane = lax.broadcasted_iota(jnp.int32, v.shape, 1)
    return jnp.where(lane == 0, 0.0, pltpu.roll(v, 1, 1))


def next_z(v):
    row = lax.broadcasted_iota(jnp.int32, v.shape, 0)
    return jnp.where(row == v.shape[0] - 1, 0.0, pltpu.roll(v, v.shape[0] - 1, 0))


def prior_z(v):
    row = lax.broadcasted_iota(jnp.int32, v.shape, 0)
    return jnp.where(row == 0, 0.0, pltpu.roll(v, 1, 0))


def yee_kernel(
    inverse_hbm, forward_hbm, adjoint_hbm, swave_hbm, sprofile_hbm, awave_hbm, aprofile_hbm, splane_hbm, mplane_hbm,
    forward_out, adjoint_out, local_out,
    state, inverse, waves, profiles, planes, sources, partial, ghost_e, ghost_p, acc, local,
    load_sem, small_sem, e_send, e_recv, p_send, p_recv, out_sem,
):
    count = lax.axis_size("slab")
    me = lax.axis_index("slab")
    right, left = lax.rem(me + 1, count), lax.rem(me + count - 1, count)
    is_last = me == count - 1
    is_first = me == 0
    rows = state.shape[2]
    top = rows - 1
    c = courant

    barrier = pltpu.get_barrier_semaphore()
    for neighbour in (left, right):
        pl.semaphore_signal(
            barrier, inc=1, device_id={"slab": neighbour}, device_id_type=pl.DeviceIdType.MESH
        )

    loads = [
        pltpu.make_async_copy(forward_hbm.at[0], state.at[0], load_sem.at[0]),
        pltpu.make_async_copy(adjoint_hbm.at[0], state.at[1], load_sem.at[1]),
        pltpu.make_async_copy(inverse_hbm, inverse, load_sem.at[2]),
    ]
    smalls = [
        pltpu.make_async_copy(swave_hbm, waves.at[0], small_sem.at[0]),
        pltpu.make_async_copy(awave_hbm, waves.at[1], small_sem.at[1]),
        pltpu.make_async_copy(sprofile_hbm, profiles.at[0], small_sem.at[2]),
        pltpu.make_async_copy(aprofile_hbm, profiles.at[1], small_sem.at[3]),
        pltpu.make_async_copy(splane_hbm, planes.at[0], small_sem.at[4]),
        pltpu.make_async_copy(mplane_hbm, planes.at[1], small_sem.at[5]),
    ]
    for copy in loads + smalls:
        copy.start()

    def send_e(run, turn):
        return pltpu.make_async_remote_copy(
            src_ref=state.at[run, pl.ds(1, 2), 0],
            dst_ref=ghost_e.at[turn, run],
            send_sem=e_send.at[turn, run],
            recv_sem=e_recv.at[turn, run],
            device_id={"slab": left},
            device_id_type=pl.DeviceIdType.MESH,
        )

    def send_p(run, turn):
        return pltpu.make_async_remote_copy(
            src_ref=partial.at[turn, run],
            dst_ref=ghost_p.at[turn, run],
            send_sem=p_send.at[turn, run],
            recv_sem=p_recv.at[turn, run],
            device_id={"slab": right},
            device_id_type=pl.DeviceIdType.MESH,
        )

    def make_partial(run, turn):
        elec_x, elec_y, elec_z = (state[run, comp, top] for comp in range(3))
        partial[turn, run, 0] = state[run, 4, top] - c * (next_z(elec_x) - elec_x + elec_z)
        partial[turn, run, 1] = state[run, 5, top] + c * (elec_y + next_y(elec_x) - elec_x)

    def magnetic_x(run, row):
        elec_y, elec_z = state[run, 1, row], state[run, 2, row]
        state[run, 3, row] = state[run, 3, row] - c * (
            next_y(elec_z) - elec_z - (next_z(elec_y) - elec_y)
        )

    def magnetic_row(run, row):
        magnetic_x(run, row)
        elec_x, elec_y, elec_z = (state[run, comp, row] for comp in range(3))
        state[run, 4, row] = state[run, 4, row] - c * (
            next_z(elec_x) - elec_x - (state[run, 2, row + 1] - elec_z)
        )
        state[run, 5, row] = state[run, 5, row] - c * (
            state[run, 1, row + 1] - elec_y - (next_y(elec_x) - elec_x)
        )

    def electric_row(run, row, turn, prior_hy, prior_hz):
        magn_x, magn_y, magn_z = (state[run, comp, row] for comp in range(3, 6))
        scaled = c * inverse[row]
        source = sources[run] * waves[run, :, turn : turn + 1]
        elec_x = (
            state[run, 0, row]
            + scaled * (magn_z - prior_y(magn_z) - (magn_y - prior_z(magn_y)))
            + source
        )
        elec_y = state[run, 1, row] + scaled * (magn_x - prior_z(magn_x) - (magn_z - prior_hz))
        elec_z = state[run, 2, row] + scaled * (magn_y - prior_hy - (magn_x - prior_y(magn_x)))
        state[run, 0, row] = elec_x
        state[run, 1, row] = elec_y
        state[run, 2, row] = elec_z
        if run == 1:
            total = (
                elec_x * state[0, 0, row] + elec_y * state[0, 1, row] + elec_z * state[0, 2, row]
            )
            folded = total[0:8] + total[8:16] + total[16:24]
            if turn == 0:
                acc[row] = folded
            else:
                acc[row] = acc[row] + folded

    def interior(run, turn):
        magnetic_row(run, 0)

        @pl.loop(1, top)
        def _(row):
            magnetic_row(run, row)
            electric_row(run, row, turn, state[run, 4, row - 1], state[run, 5, row - 1])

        magnetic_x(run, top)

    def boundary(run, turn):
        send_e(run, turn).wait_recv()
        state[run, 4, top] = partial[turn, run, 0] + c * jnp.where(
            is_last, 0.0, ghost_e[turn, run, 1]
        )
        state[run, 5, top] = partial[turn, run, 1] - c * jnp.where(
            is_last, 0.0, ghost_e[turn, run, 0]
        )
        electric_row(run, top, turn, state[run, 4, top - 1], state[run, 5, top - 1])
        if turn < STEPS - 1:
            make_partial(run, turn + 1)
            send_p(run, turn + 1).start()
        send_p(run, turn).wait_recv()
        prior_hy = jnp.where(is_first, 0.0, ghost_p[turn, run, 0] + c * state[run, 2, 0])
        prior_hz = jnp.where(is_first, 0.0, ghost_p[turn, run, 1] - c * state[run, 1, 0])
        send_e(run, turn).wait_send()
        electric_row(run, 0, turn, prior_hy, prior_hz)
        if turn < STEPS - 1:
            send_e(run, turn + 1).start()

    loads[0].wait()
    make_partial(0, 0)
    pl.semaphore_wait(barrier, 2)
    send_e(0, 0).start()
    send_p(0, 0).start()
    loads[1].wait()
    make_partial(1, 0)
    send_e(1, 0).start()
    send_p(1, 0).start()
    for copy in smalls:
        copy.wait()
    loads[2].wait()
    for run in range(2):
        level = lax.broadcasted_iota(jnp.int32, (NZ, NY), 0)
        hit = level == planes[run]
        sources[run] = jnp.where(hit, jnp.broadcast_to(profiles[run], (NZ, NY)), 0.0)

    interior(0, 0)
    interior(1, 0)
    for turn in range(STEPS):
        for run in range(2):
            boundary(run, turn)
            if turn < STEPS - 1:
                interior(run, turn + 1)

    outs = [
        pltpu.make_async_copy(state.at[0], forward_out.at[0], out_sem.at[0]),
        pltpu.make_async_copy(state.at[1], adjoint_out.at[0], out_sem.at[1]),
    ]
    for copy in outs:
        copy.start()
    local[...] = jnp.sum(acc[...], axis=1)
    last = pltpu.make_async_copy(local, local_out, out_sem.at[2])
    last.start()
    for turn in range(STEPS):
        for run in range(2):
            send_p(run, turn).wait_send()
    for copy in outs + [last]:
        copy.wait()


def yee(inverse, forward, adjoint, swave, sprofile, awave, aprofile, splane, mplane):
    rows = forward.shape[2]
    plane = (rows, NZ, NY)
    return pl.pallas_call(
        yee_kernel,
        out_shape=(
            jax.ShapeDtypeStruct(forward.shape, jnp.float32),
            jax.ShapeDtypeStruct(adjoint.shape, jnp.float32),
            jax.ShapeDtypeStruct((rows, NY), jnp.float32),
        ),
        in_specs=[pl.BlockSpec(memory_space=pl.ANY)] * 9,
        out_specs=[pl.BlockSpec(memory_space=pl.ANY)] * 3,
        scratch_shapes=[
            pltpu.VMEM((2, 6) + plane, jnp.float32),
            pltpu.VMEM(plane, jnp.float32),
            pltpu.VMEM((2, 1, STEPS), jnp.float32),
            pltpu.VMEM((2, 1, NY), jnp.float32),
            pltpu.VMEM((2, 1, 1), jnp.int32),
            pltpu.VMEM((2, NZ, NY), jnp.float32),
            pltpu.VMEM((STEPS, 2, 2, NZ, NY), jnp.float32),
            pltpu.VMEM((STEPS, 2, 2, NZ, NY), jnp.float32),
            pltpu.VMEM((STEPS, 2, 2, NZ, NY), jnp.float32),
            pltpu.VMEM((rows, 8, NY), jnp.float32),
            pltpu.VMEM((rows, NY), jnp.float32),
            pltpu.SemaphoreType.DMA((3,)),
            pltpu.SemaphoreType.DMA((6,)),
            pltpu.SemaphoreType.DMA((STEPS, 2)),
            pltpu.SemaphoreType.DMA((STEPS, 2)),
            pltpu.SemaphoreType.DMA((STEPS, 2)),
            pltpu.SemaphoreType.DMA((STEPS, 2)),
            pltpu.SemaphoreType.DMA((3,)),
        ],
        compiler_params=pltpu.CompilerParams(collective_id=0, has_side_effects=True),
        name="yee",
    )(inverse, forward, adjoint, swave, sprofile, awave, aprofile, splane, mplane)


def over_pieces(shard, axis):
    return lax.all_gather(shard, axis).sum(0)


def padded_2(cells, sides, width):
    for axis, dim in sides:
        count = lax.axis_size(axis)
        ends = count - 1
        head = lax.slice_in_dim(cells, 0, width, axis=dim)
        tail = lax.slice_in_dim(cells, cells.shape[dim] - width, cells.shape[dim], axis=dim)
        cells = jnp.concatenate(
            [
                lax.ppermute(tail, axis, [(i, (i + 1) % count) for i in range(ends)]),
                cells,
                lax.ppermute(head, axis, [((i + 1) % count, i) for i in range(ends)]),
            ],
            axis=dim,
        )
    return cells


def on_device(
    inverse_permittivity,
    forward_fields,
    adjoint_fields,
    source_wave,
    source_profile,
    adjoint_wave,
    adjoint_profile,
    source_plane,
    monitor_plane,
    radius_map,
    design_mask,
    design_density,
):
    forward_out, adjoint_out, local = yee(
        inverse_permittivity,
        forward_fields,
        adjoint_fields,
        source_wave,
        source_profile,
        adjoint_wave,
        adjoint_profile,
        source_plane.reshape(1, 1),
        monitor_plane.reshape(1, 1),
    )
    sent = over_pieces(local, "freq").T
    tiles = lax.all_to_all(sent, "slab", split_axis=0, concat_axis=1, tiled=True)
    tile_rows = tiles.shape[0]
    width = design_density.shape[1]
    columns = width // radius_map.shape[1]
    radius = jnp.repeat(radius_map, columns, axis=1).astype(jnp.float32)
    chosen = jnp.repeat(design_mask, columns, axis=1).astype(jnp.float32)
    scale = step_size / math.sqrt(3 * STEPS * NZ * FREQS)
    updated = design_density + scale * chosen * tiles
    rim = padded_2(updated, (("slab", 0),), RMAX)
    padded = jnp.pad(rim, ((0, 0), (RMAX, RMAX)))
    global_y = (
        lax.axis_index("slab") * tile_rows
        - RMAX
        + jnp.arange(tile_rows + 2 * RMAX, dtype=jnp.int32)
    )
    inside_y = ((global_y >= 0) & (global_y < NY)).astype(jnp.float32)
    inside_x = jnp.pad(jnp.ones((width,), jnp.float32), RMAX)
    inside = inside_y[:, None] * inside_x[None, :]
    numerator = jnp.zeros((tile_rows, width), jnp.float32)
    weight_total = jnp.zeros((tile_rows, width), jnp.float32)
    for offset_y in range(2 * RMAX + 1):
        for offset_x in range(2 * RMAX + 1):
            distance = jnp.sqrt(
                jnp.asarray((offset_y - RMAX) ** 2 + (offset_x - RMAX) ** 2, jnp.float32)
            )
            weight = jnp.maximum(radius - distance, 0.0)
            piece = padded[offset_y : offset_y + tile_rows, offset_x : offset_x + width]
            present = inside[offset_y : offset_y + tile_rows, offset_x : offset_x + width]
            numerator = numerator + weight * present * piece
            weight_total = weight_total + weight * present
    filtered = numerator / weight_total
    base = math.tanh(sharpness * midpoint)
    projected = (base + jnp.tanh(sharpness * (filtered - midpoint))) / (
        base + math.tanh(sharpness * (1.0 - midpoint))
    )
    return (forward_out, adjoint_out, projected)


def solution(mesh):
    return jax.shard_map(
        on_device,
        mesh=mesh,
        in_specs=(
            P("slab", None, None),
            P("freq", None, "slab", None, None),
            P("freq", None, "slab", None, None),
            P("freq", None),
            P("freq", None),
            P("freq", None),
            P("freq", None),
            P("freq"),
            P("freq"),
            P("slab", None),
            P("slab", None),
            P("slab", None),
        ),
        out_specs=(
            P("freq", None, "slab", None, None),
            P("freq", None, "slab", None, None),
            P("slab", None),
        ),
        check_vma=False,
    )
```

```python
import math

import jax
import jax.numpy as jnp
from jax import lax
from jax.experimental import pallas as pl
from jax.experimental.pallas import tpu as pltpu
from jax.sharding import PartitionSpec as P

NY = 512
NZ = 24
FREQS = 4
STEPS = 3
RMAX = 4


courant = 0.5
sharpness = 4.0
midpoint = 0.5
step_size = 0.3


def next_y(v):
    lane = lax.broadcasted_iota(jnp.int32, v.shape, 1)
    return jnp.where(lane == v.shape[1] - 1, 0.0, pltpu.roll(v, v.shape[1] - 1, 1))


def prior_y(v):
    lane = lax.broadcasted_iota(jnp.int32, v.shape, 1)
    return jnp.where(lane == 0, 0.0, pltpu.roll(v, 1, 1))


def next_z(v):
    row = lax.broadcasted_iota(jnp.int32, v.shape, 0)
    return jnp.where(row == v.shape[0] - 1, 0.0, pltpu.roll(v, v.shape[0] - 1, 0))


def prior_z(v):
    row = lax.broadcasted_iota(jnp.int32, v.shape, 0)
    return jnp.where(row == 0, 0.0, pltpu.roll(v, 1, 0))


def yee_kernel(
    inverse_hbm, forward_hbm, adjoint_hbm, swave_hbm, sprofile_hbm, awave_hbm, aprofile_hbm, splane_hbm, mplane_hbm,
    radius_hbm, mask_hbm, density_hbm,
    forward_out, adjoint_out, projected_out,
    state, inverse, waves, profiles, planes, sources, partial, ghost_e, ghost_p, acc,
    radius, mask, design, beside, weights, gathered, outgoing, incoming, projected,
    load_sem, small_sem, e_send, e_recv, p_send, p_recv, out_sem,
    greet_sem, beside_send, beside_recv, freq_send, freq_recv, tile_send, tile_recv,
):
    count = lax.axis_size("slab")
    me = lax.axis_index("slab")
    right, left = lax.rem(me + 1, count), lax.rem(me + count - 1, count)
    is_last = me == count - 1
    is_first = me == 0
    rows = state.shape[2]
    top = rows - 1
    c = courant

    group = lax.axis_index("freq")
    groups = lax.axis_size("freq")
    barrier = pltpu.get_barrier_semaphore()
    for neighbour in (left, right):
        pl.semaphore_signal(
            barrier, inc=1, device_id={"slab": neighbour}, device_id_type=pl.DeviceIdType.MESH
        )
    for ahead in range(1, groups):
        pl.semaphore_signal(
            barrier,
            inc=1,
            device_id={"freq": lax.rem(group + ahead, groups)},
            device_id_type=pl.DeviceIdType.MESH,
        )

    loads = [
        pltpu.make_async_copy(forward_hbm.at[0], state.at[0], load_sem.at[0]),
        pltpu.make_async_copy(adjoint_hbm.at[0], state.at[1], load_sem.at[1]),
        pltpu.make_async_copy(inverse_hbm, inverse, load_sem.at[2]),
    ]
    smalls = [
        pltpu.make_async_copy(swave_hbm, waves.at[0], small_sem.at[0]),
        pltpu.make_async_copy(awave_hbm, waves.at[1], small_sem.at[1]),
        pltpu.make_async_copy(sprofile_hbm, profiles.at[0], small_sem.at[2]),
        pltpu.make_async_copy(aprofile_hbm, profiles.at[1], small_sem.at[3]),
        pltpu.make_async_copy(splane_hbm, planes.at[0], small_sem.at[4]),
        pltpu.make_async_copy(mplane_hbm, planes.at[1], small_sem.at[5]),
        pltpu.make_async_copy(radius_hbm, radius, small_sem.at[6]),
        pltpu.make_async_copy(mask_hbm, mask, small_sem.at[7]),
        pltpu.make_async_copy(density_hbm, design.at[0], small_sem.at[8]),
    ]
    for copy in loads + smalls:
        copy.start()

    def send_e(run, turn):
        return pltpu.make_async_remote_copy(
            src_ref=state.at[run, pl.ds(1, 2), 0],
            dst_ref=ghost_e.at[turn, run],
            send_sem=e_send.at[turn, run],
            recv_sem=e_recv.at[turn, run],
            device_id={"slab": left},
            device_id_type=pl.DeviceIdType.MESH,
        )

    def send_p(run, turn):
        return pltpu.make_async_remote_copy(
            src_ref=partial.at[turn, run],
            dst_ref=ghost_p.at[turn, run],
            send_sem=p_send.at[turn, run],
            recv_sem=p_recv.at[turn, run],
            device_id={"slab": right},
            device_id_type=pl.DeviceIdType.MESH,
        )

    def make_partial(run, turn):
        elec_x, elec_y, elec_z = (state[run, comp, top] for comp in range(3))
        partial[turn, run, 0] = state[run, 4, top] - c * (next_z(elec_x) - elec_x + elec_z)
        partial[turn, run, 1] = state[run, 5, top] + c * (elec_y + next_y(elec_x) - elec_x)

    def magnetic_x(run, row):
        elec_y, elec_z = state[run, 1, row], state[run, 2, row]
        state[run, 3, row] = state[run, 3, row] - c * (
            next_y(elec_z) - elec_z - (next_z(elec_y) - elec_y)
        )

    def magnetic_row(run, row):
        magnetic_x(run, row)
        elec_x, elec_y, elec_z = (state[run, comp, row] for comp in range(3))
        state[run, 4, row] = state[run, 4, row] - c * (
            next_z(elec_x) - elec_x - (state[run, 2, row + 1] - elec_z)
        )
        state[run, 5, row] = state[run, 5, row] - c * (
            state[run, 1, row + 1] - elec_y - (next_y(elec_x) - elec_x)
        )

    def electric_row(run, row, turn, prior_hy, prior_hz):
        magn_x, magn_y, magn_z = (state[run, comp, row] for comp in range(3, 6))
        scaled = c * inverse[row]
        source = sources[run] * waves[run, :, turn : turn + 1]
        elec_x = (
            state[run, 0, row]
            + scaled * (magn_z - prior_y(magn_z) - (magn_y - prior_z(magn_y)))
            + source
        )
        elec_y = state[run, 1, row] + scaled * (magn_x - prior_z(magn_x) - (magn_z - prior_hz))
        elec_z = state[run, 2, row] + scaled * (magn_y - prior_hy - (magn_x - prior_y(magn_x)))
        state[run, 0, row] = elec_x
        state[run, 1, row] = elec_y
        state[run, 2, row] = elec_z
        if run == 1:
            total = (
                elec_x * state[0, 0, row] + elec_y * state[0, 1, row] + elec_z * state[0, 2, row]
            )
            folded = total[0:8] + total[8:16] + total[16:24]
            if turn == 0:
                acc[row] = folded
            else:
                acc[row] = acc[row] + folded

    def interior(run, turn):
        magnetic_row(run, 0)

        @pl.loop(1, top)
        def _(row):
            magnetic_row(run, row)
            electric_row(run, row, turn, state[run, 4, row - 1], state[run, 5, row - 1])

        magnetic_x(run, top)

    def boundary(run, turn):
        send_e(run, turn).wait_recv()
        state[run, 4, top] = partial[turn, run, 0] + c * jnp.where(
            is_last, 0.0, ghost_e[turn, run, 1]
        )
        state[run, 5, top] = partial[turn, run, 1] - c * jnp.where(
            is_last, 0.0, ghost_e[turn, run, 0]
        )
        electric_row(run, top, turn, state[run, 4, top - 1], state[run, 5, top - 1])
        if turn < STEPS - 1:
            make_partial(run, turn + 1)
            send_p(run, turn + 1).start()
        send_p(run, turn).wait_recv()
        prior_hy = jnp.where(is_first, 0.0, ghost_p[turn, run, 0] + c * state[run, 2, 0])
        prior_hz = jnp.where(is_first, 0.0, ghost_p[turn, run, 1] - c * state[run, 1, 0])
        send_e(run, turn).wait_send()
        electric_row(run, 0, turn, prior_hy, prior_hz)
        if turn < STEPS - 1:
            send_e(run, turn + 1).start()

    def greet(level):
        for there in (me + count - (1 << level), me + (1 << level)):
            pl.semaphore_signal(
                greet_sem.at[level],
                inc=1,
                device_id={"slab": lax.rem(there, count)},
                device_id_type=pl.DeviceIdType.MESH,
            )

    levels = 0
    while (2 << levels) < count:
        levels += 1

    def greeted(level):
        if level < levels:
            pl.semaphore_wait(greet_sem.at[level], 2)
            if level + 1 < levels:
                greet(level + 1)

    def send_beside(side):
        return pltpu.make_async_remote_copy(
            src_ref=design,
            dst_ref=beside.at[side],
            send_sem=beside_send.at[side],
            recv_sem=beside_recv.at[side],
            device_id={"slab": (right, left)[side]},
            device_id_type=pl.DeviceIdType.MESH,
        )

    def send_freq(ahead):
        return pltpu.make_async_remote_copy(
            src_ref=gathered.at[group],
            dst_ref=gathered.at[group],
            send_sem=freq_send.at[ahead - 1],
            recv_sem=freq_recv.at[ahead - 1],
            device_id={"freq": lax.rem(group + ahead, groups)},
            device_id_type=pl.DeviceIdType.MESH,
        )

    def send_tile(ahead):
        there = lax.rem(me + ahead, count)
        return pltpu.make_async_remote_copy(
            src_ref=outgoing.at[there],
            dst_ref=incoming.at[me],
            send_sem=tile_send,
            recv_sem=tile_recv,
            device_id={"slab": there},
            device_id_type=pl.DeviceIdType.MESH,
        )

    loads[0].wait()
    make_partial(0, 0)
    pl.semaphore_wait(barrier, 2 + groups - 1)
    send_e(0, 0).start()
    send_p(0, 0).start()
    if levels > 0:
        greet(0)
    loads[1].wait()
    make_partial(1, 0)
    send_e(1, 0).start()
    send_p(1, 0).start()
    for copy in smalls:
        copy.wait()
    loads[2].wait()
    for run in range(2):
        level = lax.broadcasted_iota(jnp.int32, sources.shape[1:], 0)
        hit = level == planes[run]
        sources[run] = jnp.where(hit, jnp.broadcast_to(profiles[run], hit.shape), 0.0)

    width = density_hbm.shape[1]
    scale = step_size / math.sqrt(3 * STEPS * NZ * FREQS)
    tile_x = width // radius.shape[1]
    column = lax.broadcasted_iota(jnp.int32, (8, width), 1)
    line = lax.broadcasted_iota(jnp.int32, (8, width), 0)

    def spread(table):
        wide = jnp.zeros((8, width), jnp.float32)
        for tile in range(table.shape[1]):
            value = jnp.broadcast_to(table[:, tile : tile + 1], (8, width)).astype(jnp.float32)
            wide = jnp.where(column // tile_x == tile, value, wide)
        return wide

    design[1] = scale * spread(mask)
    reach = spread(radius)
    rim_inside = ((line < 4) & (me < count - 1)) | ((line >= 4) & (me > 0))

    def shift_x(v, by):
        if by == 0:
            return v
        inside = (column + by >= 0) & (column + by < width)
        return jnp.where(inside, pltpu.roll(v, (width - by) % width, 1), 0.0)

    def shift_y(own, rim, by):
        if by == 0:
            return own
        mixed = jnp.where(line < by, rim, own) if by > 0 else jnp.where(line >= 8 + by, rim, own)
        return pltpu.roll(mixed, (8 - by) % 8, 0)

    def rings(own, rim):
        totals = {}
        for up in range(RMAX + 1):
            piece = shift_y(own, rim, up)
            if up:
                piece = piece + shift_y(own, rim, -up)
            for over in range(RMAX + 1):
                both = shift_x(piece, over)
                if over:
                    both = both + shift_x(piece, -over)
                key = up * up + over * over
                totals[key] = totals[key] + both if key in totals else both
        return totals

    def prepare_weights():
        counts = rings(jnp.ones((8, width), jnp.float32), jnp.where(rim_inside, 1.0, 0.0))
        total = jnp.zeros((8, width), jnp.float32)
        for key in counts:
            total = total + jnp.maximum(reach - math.sqrt(key), 0.0) * counts[key]
        for place, key in enumerate(sorted(counts)):
            weights[place] = jnp.maximum(reach - math.sqrt(key), 0.0) / total

    interior(0, 0)
    greeted(0)
    interior(1, 0)
    greeted(1)
    for turn in range(STEPS):
        for run in range(2):
            boundary(run, turn)
            if turn < STEPS - 1:
                interior(run, turn + 1)
            greeted(2 + 2 * turn + run)
        if turn == STEPS - 2:
            send_beside(0).start()
            send_beside(1).start()
            prepare_weights()

    gathered[group] = jnp.sum(acc[...], axis=1)
    for ahead in range(1, groups):
        send_freq(ahead).start()
    outs = [
        pltpu.make_async_copy(state.at[0], forward_out.at[0], out_sem.at[0]),
        pltpu.make_async_copy(state.at[1], adjoint_out.at[0], out_sem.at[1]),
    ]
    for copy in outs:
        copy.start()
    for ahead in range(1, groups):
        send_freq(ahead).wait_recv()
    whole = gathered[0]
    for index in range(1, groups):
        whole = whole + gathered[index]

    sub = lax.broadcasted_iota(jnp.int32, (8, 128), 0)
    lane = lax.broadcasted_iota(jnp.int32, (8, 128), 1)

    def swap_bits(v, sub_bit, lane_bit):
        high, low = (sub >> sub_bit) & 1, (lane >> lane_bit) & 1
        rows_by, lanes_by = 1 << sub_bit, 1 << lane_bit
        from_high = pltpu.roll(pltpu.roll(v, 8 - rows_by, 0), lanes_by, 1)
        from_low = pltpu.roll(pltpu.roll(v, rows_by, 0), 128 - lanes_by, 1)
        return jnp.where(high == low, v, jnp.where(high == 0, from_high, from_low))

    strips = []
    for block in range(width // 128):
        v = whole[:, 128 * block : 128 * (block + 1)]
        for bit in range(3):
            v = swap_bits(v, bit, bit)
        for bit in range(3):
            v = swap_bits(v, bit, 3 + bit)
        strips += [v, pltpu.roll(v, 64, 1)]
    pieces = len(strips)
    for index in range(pieces):
        mine, above, below = strips[index], strips[(index + 1) % pieces], strips[index - 1]
        upper = pltpu.roll(jnp.where(sub == 0, above, mine), 7, 0)
        lower = pltpu.roll(jnp.where(sub == 7, below, mine), 1, 0)
        rim = jnp.where(lane < 32, upper, lower)
        packed = jnp.where(lane < 64, mine, pltpu.roll(rim, 64, 1))
        for row in range(8):
            outgoing[8 * index + row] = packed[row : row + 1]
    incoming[me] = outgoing[me]

    @pl.loop(1, count)
    def _(ahead):
        send_tile(ahead).start()

    for side in range(2):
        send_beside(side).wait_recv()
    rim_density = jnp.where(line < 4, beside[1, 0], beside[0, 0])
    rim_scale = jnp.where(line < 4, beside[1, 1], beside[0, 1])
    pltpu.make_async_copy(
        incoming.at[pl.ds(0, count - 1)], incoming.at[pl.ds(0, count - 1)], tile_recv
    ).wait()
    own_parts, rim_parts = [], []
    for index in range(0, pieces, 2):
        halves = []
        for half in (index, index + 1):
            v = jnp.concatenate([incoming[8 * half + row] for row in range(8)], axis=0)
            for bit in range(3):
                v = swap_bits(v, bit, 3 + bit)
            halves.append(v)
        own_parts.append(jnp.where(lane < 64, halves[0], pltpu.roll(halves[1], 64, 1)))
        rim_parts.append(jnp.where(lane < 64, pltpu.roll(halves[0], 64, 1), halves[1]))
    own = design[0] + design[1] * jnp.concatenate(own_parts, axis=1)
    rim = rim_density + rim_scale * jnp.concatenate(rim_parts, axis=1)
    sums = rings(own, jnp.where(rim_inside, rim, 0.0))
    filtered = jnp.zeros((8, width), jnp.float32)
    for place, key in enumerate(sorted(sums)):
        filtered = filtered + weights[place] * sums[key]
    base = math.tanh(sharpness * midpoint)
    projected[...] = (base + jnp.tanh(sharpness * (filtered - midpoint))) / (
        base + math.tanh(sharpness * (1.0 - midpoint))
    )
    last = pltpu.make_async_copy(projected, projected_out, out_sem.at[2])
    last.start()
    for turn in range(STEPS):
        for run in range(2):
            send_p(run, turn).wait_send()
    for side in range(2):
        send_beside(side).wait_send()
    for ahead in range(1, groups):
        send_freq(ahead).wait_send()
    pltpu.make_async_copy(
        incoming.at[pl.ds(0, count - 1)], incoming.at[pl.ds(0, count - 1)], tile_send
    ).wait()
    for copy in outs + [last]:
        copy.wait()


def yee(*operands):
    forward = operands[1]
    density = operands[11]
    rows, high, wide = forward.shape[2:]
    plane = (rows, high, wide)
    width = density.shape[1]
    count = lax.axis_size("slab")
    groups = lax.axis_size("freq")
    return pl.pallas_call(
        yee_kernel,
        out_shape=(
            jax.ShapeDtypeStruct(forward.shape, jnp.float32),
            jax.ShapeDtypeStruct(forward.shape, jnp.float32),
            jax.ShapeDtypeStruct(density.shape, jnp.float32),
        ),
        in_specs=[pl.BlockSpec(memory_space=pl.ANY)] * 12,
        out_specs=[pl.BlockSpec(memory_space=pl.ANY)] * 3,
        scratch_shapes=[
            pltpu.VMEM((2, 6) + plane, jnp.float32),
            pltpu.VMEM(plane, jnp.float32),
            pltpu.VMEM((2, 1, STEPS), jnp.float32),
            pltpu.VMEM((2, 1, wide), jnp.float32),
            pltpu.VMEM((2, 1, 1), jnp.int32),
            pltpu.VMEM((2, high, wide), jnp.float32),
            pltpu.VMEM((STEPS, 2, 2, high, wide), jnp.float32),
            pltpu.VMEM((STEPS, 2, 2, high, wide), jnp.float32),
            pltpu.VMEM((STEPS, 2, 2, high, wide), jnp.float32),
            pltpu.VMEM((rows, 8, wide), jnp.float32),
            pltpu.VMEM(operands[9].shape, jnp.int32),
            pltpu.VMEM(operands[10].shape, jnp.int32),
            pltpu.VMEM((2, 8, width), jnp.float32),
            pltpu.VMEM((2, 2, 8, width), jnp.float32),
            pltpu.VMEM((15, 8, width), jnp.float32),
            pltpu.VMEM((groups, rows, wide), jnp.float32),
            pltpu.VMEM((count, 1, 128), jnp.float32),
            pltpu.VMEM((count, 1, 128), jnp.float32),
            pltpu.VMEM((8, width), jnp.float32),
            pltpu.SemaphoreType.DMA((3,)),
            pltpu.SemaphoreType.DMA((9,)),
            pltpu.SemaphoreType.DMA((STEPS, 2)),
            pltpu.SemaphoreType.DMA((STEPS, 2)),
            pltpu.SemaphoreType.DMA((STEPS, 2)),
            pltpu.SemaphoreType.DMA((STEPS, 2)),
            pltpu.SemaphoreType.DMA((3,)),
            pltpu.SemaphoreType.REGULAR((8,)),
            pltpu.SemaphoreType.DMA((2,)),
            pltpu.SemaphoreType.DMA((2,)),
            pltpu.SemaphoreType.DMA((3,)),
            pltpu.SemaphoreType.DMA((3,)),
            pltpu.SemaphoreType.DMA,
            pltpu.SemaphoreType.DMA,
        ],
        compiler_params=pltpu.CompilerParams(collective_id=0, has_side_effects=True),
        name="yee",
    )(*operands)


def on_device(
    inverse_permittivity,
    forward_fields,
    adjoint_fields,
    source_wave,
    source_profile,
    adjoint_wave,
    adjoint_profile,
    source_plane,
    monitor_plane,
    radius_map,
    design_mask,
    design_density,
):
    return yee(
        inverse_permittivity,
        forward_fields,
        adjoint_fields,
        source_wave,
        source_profile,
        adjoint_wave,
        adjoint_profile,
        source_plane.reshape(1, 1),
        monitor_plane.reshape(1, 1),
        radius_map,
        design_mask,
        design_density,
    )


def solution(mesh):
    return jax.shard_map(
        on_device,
        mesh=mesh,
        in_specs=(
            P("slab", None, None),
            P("freq", None, "slab", None, None),
            P("freq", None, "slab", None, None),
            P("freq", None),
            P("freq", None),
            P("freq", None),
            P("freq", None),
            P("freq"),
            P("freq"),
            P("slab", None),
            P("slab", None),
            P("slab", None),
        ),
        out_specs=(
            P("freq", None, "slab", None, None),
            P("freq", None, "slab", None, None),
            P("slab", None),
        ),
        check_vma=False,
    )
```

```python
import math

import jax
import jax.numpy as jnp
from jax import lax
from jax.experimental import pallas as pl
from jax.experimental.pallas import tpu as pltpu
from jax.sharding import PartitionSpec as P

NY = 512
NZ = 24
FREQS = 4
STEPS = 3
RMAX = 4
SIDE_X, SIDE_Z, SIDE_Y = 4, 8, 2


courant = 0.5
sharpness = 4.0
midpoint = 0.5
step_size = 0.3


def next_y(v):
    lane = lax.broadcasted_iota(jnp.int32, v.shape, 1)
    return jnp.where(lane == v.shape[1] - 1, 0.0, pltpu.roll(v, v.shape[1] - 1, 1))


def prior_y(v):
    lane = lax.broadcasted_iota(jnp.int32, v.shape, 1)
    return jnp.where(lane == 0, 0.0, pltpu.roll(v, 1, 1))


def next_z(v):
    row = lax.broadcasted_iota(jnp.int32, v.shape, 0)
    return jnp.where(row == v.shape[0] - 1, 0.0, pltpu.roll(v, v.shape[0] - 1, 0))


def prior_z(v):
    row = lax.broadcasted_iota(jnp.int32, v.shape, 0)
    return jnp.where(row == 0, 0.0, pltpu.roll(v, 1, 0))


def yee_kernel(
    inverse_hbm, forward_hbm, adjoint_hbm, swave_hbm, sprofile_hbm, awave_hbm, aprofile_hbm, planes_hbm,
    radius_hbm, mask_hbm, density_hbm,
    state, projected,
    inverse, waves, profiles, planes, sources, partial, ghost_e, ghost_p, acc,
    radius, mask, design, beside, weights, outgoing, incoming,
    load_sem, small_sem, e_send, e_recv, p_send, p_recv,
    greet_sem, beside_send, beside_recv, tile_send, tile_recv,
):
    count = lax.axis_size("slab")
    me = lax.axis_index("slab")
    right, left = lax.rem(me + 1, count), lax.rem(me + count - 1, count)
    is_last = me == count - 1
    is_first = me == 0
    rows = state.shape[2]
    top = rows - 1
    c = courant

    group = lax.axis_index("freq")
    groups = lax.axis_size("freq")
    at_x, at_z, at_y = me % SIDE_X, (me // SIDE_X) % SIDE_Z, me // (SIDE_X * SIDE_Z)

    def device(by_x=0, by_z=0, by_y=0, by_far=0, by_core=0):
        far, core = (group // 2 + by_far) % 2, (group % 2 + by_core) % 2
        slab = (
            (at_y + by_y) % SIDE_Y * SIDE_Z + (at_z + by_z) % SIDE_Z
        ) * SIDE_X + (at_x + by_x) % SIDE_X
        return {"freq": far * 2 + core, "slab": slab}

    line_x = [dict(by_x=by) for by in range(1, SIDE_X)]
    line_y = [
        dict(by_y=y, by_far=far, by_core=core)
        for y in range(2)
        for far in range(2)
        for core in range(2)
        if y + far + core
    ]
    near_z = [dict(by_z=1), dict(by_z=SIDE_Z - 1)]
    next_z_two = [dict(by_z=2), dict(by_z=SIDE_Z - 2)]
    rounds = [near_z, next_z_two, line_x, line_y]

    def signal(semaphore, partners):
        for partner in partners:
            pl.semaphore_signal(
                semaphore,
                inc=1,
                device_id=device(**partner),
                device_id_type=pl.DeviceIdType.MESH,
            )

    barrier = pltpu.get_barrier_semaphore()
    for neighbour in (left, right):
        pl.semaphore_signal(
            barrier, inc=1, device_id={"slab": neighbour}, device_id_type=pl.DeviceIdType.MESH
        )
    greetings = near_z + line_x + line_y
    signal(barrier, greetings)

    def greet(level):
        signal(greet_sem.at[level], rounds[level])

    def greeted(level):
        if level < len(rounds):
            pl.semaphore_wait(greet_sem.at[level], len(rounds[level]))
            if level + 1 < len(rounds):
                greet(level + 1)

    fields = (forward_hbm, adjoint_hbm)
    edges = [
        pltpu.make_async_copy(fields[run].at[0, :, top], state.at[run, :, top], load_sem.at[run])
        for run in range(2)
    ]
    loads = [
        pltpu.make_async_copy(
            fields[run].at[0, :, pl.ds(0, top)], state.at[run, :, pl.ds(0, top)], load_sem.at[2 + run]
        )
        for run in range(2)
    ]
    medium = pltpu.make_async_copy(inverse_hbm, inverse, load_sem.at[4])
    smalls = [
        pltpu.make_async_copy(swave_hbm, waves.at[0], small_sem.at[0]),
        pltpu.make_async_copy(awave_hbm, waves.at[1], small_sem.at[1]),
        pltpu.make_async_copy(sprofile_hbm, profiles.at[0], small_sem.at[2]),
        pltpu.make_async_copy(aprofile_hbm, profiles.at[1], small_sem.at[3]),
        pltpu.make_async_copy(planes_hbm, planes, small_sem.at[4]),
        pltpu.make_async_copy(radius_hbm, radius, small_sem.at[6]),
        pltpu.make_async_copy(mask_hbm, mask, small_sem.at[7]),
        pltpu.make_async_copy(density_hbm, design.at[0], small_sem.at[8]),
    ]
    for copy in edges + [loads[0], medium, loads[1]] + smalls:
        copy.start()

    def send_e(run, turn):
        return pltpu.make_async_remote_copy(
            src_ref=state.at[run, pl.ds(1, 2), 0] if turn else fields[run].at[0, pl.ds(1, 2), 0],
            dst_ref=ghost_e.at[turn, run],
            send_sem=e_send.at[turn, run],
            recv_sem=e_recv.at[turn, run],
            device_id={"slab": left},
            device_id_type=pl.DeviceIdType.MESH,
        )

    def send_p(run, turn):
        return pltpu.make_async_remote_copy(
            src_ref=partial.at[turn, run],
            dst_ref=ghost_p.at[turn, run],
            send_sem=p_send.at[turn, run],
            recv_sem=p_recv.at[turn, run],
            device_id={"slab": right},
            device_id_type=pl.DeviceIdType.MESH,
        )

    def make_partial(run, turn):
        elec_x, elec_y, elec_z = (state[run, comp, top] for comp in range(3))
        partial[turn, run, 0] = state[run, 4, top] - c * (next_z(elec_x) - elec_x + elec_z)
        partial[turn, run, 1] = state[run, 5, top] + c * (elec_y + next_y(elec_x) - elec_x)

    def magnetic_x(run, row):
        elec_y, elec_z = state[run, 1, row], state[run, 2, row]
        state[run, 3, row] = state[run, 3, row] - c * (
            next_y(elec_z) - elec_z - (next_z(elec_y) - elec_y)
        )

    def magnetic_row(run, row):
        magnetic_x(run, row)
        elec_x, elec_y, elec_z = (state[run, comp, row] for comp in range(3))
        state[run, 4, row] = state[run, 4, row] - c * (
            next_z(elec_x) - elec_x - (state[run, 2, row + 1] - elec_z)
        )
        state[run, 5, row] = state[run, 5, row] - c * (
            state[run, 1, row + 1] - elec_y - (next_y(elec_x) - elec_x)
        )

    def electric_row(run, row, turn, prior_hy, prior_hz):
        magn_x, magn_y, magn_z = (state[run, comp, row] for comp in range(3, 6))
        scaled = c * inverse[row]
        source = sources[run] * waves[run, :, turn : turn + 1]
        elec_x = (
            state[run, 0, row]
            + scaled * (magn_z - prior_y(magn_z) - (magn_y - prior_z(magn_y)))
            + source
        )
        elec_y = state[run, 1, row] + scaled * (magn_x - prior_z(magn_x) - (magn_z - prior_hz))
        elec_z = state[run, 2, row] + scaled * (magn_y - prior_hy - (magn_x - prior_y(magn_x)))
        state[run, 0, row] = elec_x
        state[run, 1, row] = elec_y
        state[run, 2, row] = elec_z
        if run == 1:
            total = (
                elec_x * state[0, 0, row] + elec_y * state[0, 1, row] + elec_z * state[0, 2, row]
            )
            folded = total[0:8] + total[8:16] + total[16:24]
            if turn == 0:
                acc[row] = folded
            else:
                acc[row] = acc[row] + folded

    def interior(run, turn):
        magnetic_row(run, 0)

        @pl.loop(1, top)
        def _(row):
            magnetic_row(run, row)
            electric_row(run, row, turn, state[run, 4, row - 1], state[run, 5, row - 1])

        magnetic_x(run, top)

    def boundary(run, turn):
        send_e(run, turn).wait_recv()
        state[run, 4, top] = partial[turn, run, 0] + c * jnp.where(
            is_last, 0.0, ghost_e[turn, run, 1]
        )
        state[run, 5, top] = partial[turn, run, 1] - c * jnp.where(
            is_last, 0.0, ghost_e[turn, run, 0]
        )
        electric_row(run, top, turn, state[run, 4, top - 1], state[run, 5, top - 1])
        if turn < STEPS - 1:
            make_partial(run, turn + 1)
            send_p(run, turn + 1).start()
        send_p(run, turn).wait_recv()
        prior_hy = jnp.where(is_first, 0.0, ghost_p[turn, run, 0] + c * state[run, 2, 0])
        prior_hz = jnp.where(is_first, 0.0, ghost_p[turn, run, 1] - c * state[run, 1, 0])
        send_e(run, turn).wait_send()
        electric_row(run, 0, turn, prior_hy, prior_hz)
        if turn < STEPS - 1:
            send_e(run, turn + 1).start()

    def send_beside(side):
        return pltpu.make_async_remote_copy(
            src_ref=design,
            dst_ref=beside.at[side],
            send_sem=beside_send.at[side],
            recv_sem=beside_recv.at[side],
            device_id={"slab": (right, left)[side]},
            device_id_type=pl.DeviceIdType.MESH,
        )

    def send_tile(partner):
        there = device(**partner)
        return pltpu.make_async_remote_copy(
            src_ref=outgoing.at[pl.ds(there["slab"], 1)],
            dst_ref=incoming.at[pl.ds(group * count + me, 1)],
            send_sem=tile_send,
            recv_sem=tile_recv,
            device_id=there,
            device_id_type=pl.DeviceIdType.MESH,
        )

    def hops(partner):
        side = min(partner["by_x"], SIDE_X - partner["by_x"])
        return side + (1 if partner["by_y"] else 2 * partner["by_far"])

    spokes = sorted(
        (
            dict(by_x=x, by_y=y, by_far=far, by_core=core)
            for x in range(SIDE_X)
            for y in range(SIDE_Y)
            for far in range(2)
            for core in range(2)
        ),
        key=hops,
        reverse=True,
    )

    edges[0].wait()
    make_partial(0, 0)
    pl.semaphore_wait(barrier, 2 + len(greetings))
    send_e(0, 0).start()
    send_p(0, 0).start()
    edges[1].wait()
    make_partial(1, 0)
    send_e(1, 0).start()
    send_p(1, 0).start()
    greet(0)
    for copy in smalls:
        copy.wait()
    for run in range(2):
        level = lax.broadcasted_iota(jnp.int32, sources.shape[1:], 0)
        hit = level == planes[run]
        sources[run] = jnp.where(hit, jnp.broadcast_to(profiles[run], hit.shape), 0.0)

    width = density_hbm.shape[1]
    scale = step_size / math.sqrt(3 * STEPS * NZ * FREQS)
    tile_x = width // radius.shape[1]
    column = lax.broadcasted_iota(jnp.int32, (8, width), 1)
    line = lax.broadcasted_iota(jnp.int32, (8, width), 0)

    def spread(table):
        wide = jnp.zeros((8, width), jnp.float32)
        for tile in range(table.shape[1]):
            value = jnp.broadcast_to(table[:, tile : tile + 1], (8, width)).astype(jnp.float32)
            wide = jnp.where(column // tile_x == tile, value, wide)
        return wide

    design[1] = scale * spread(mask)
    reach = spread(radius)
    rim_inside = ((line < 4) & (me < count - 1)) | ((line >= 4) & (me > 0))

    def shift_x(v, by):
        if by == 0:
            return v
        inside = (column + by >= 0) & (column + by < width)
        return jnp.where(inside, pltpu.roll(v, (width - by) % width, 1), 0.0)

    def shift_y(own, rim, by):
        if by == 0:
            return own
        mixed = jnp.where(line < by, rim, own) if by > 0 else jnp.where(line >= 8 + by, rim, own)
        return pltpu.roll(mixed, (8 - by) % 8, 0)

    def rings(own, rim):
        totals = {}
        for up in range(RMAX + 1):
            piece = shift_y(own, rim, up)
            if up:
                piece = piece + shift_y(own, rim, -up)
            for over in range(RMAX + 1):
                both = shift_x(piece, over)
                if over:
                    both = both + shift_x(piece, -over)
                key = up * up + over * over
                totals[key] = totals[key] + both if key in totals else both
        return totals

    def prepare_weights():
        counts = rings(jnp.ones((8, width), jnp.float32), jnp.where(rim_inside, 1.0, 0.0))
        total = jnp.zeros((8, width), jnp.float32)
        for key in counts:
            total = total + jnp.maximum(reach - math.sqrt(key), 0.0) * counts[key]
        for place, key in enumerate(sorted(counts)):
            weights[place] = jnp.maximum(reach - math.sqrt(key), 0.0) / total

    medium.wait()
    loads[0].wait()
    interior(0, 0)
    greeted(0)
    loads[1].wait()
    interior(1, 0)
    greeted(1)
    for turn in range(STEPS):
        for run in range(2):
            boundary(run, turn)
            if turn < STEPS - 1:
                interior(run, turn + 1)
            greeted(2 + 2 * turn + run)
        if turn == STEPS - 2:
            send_beside(0).start()
            send_beside(1).start()
            prepare_weights()

    whole = jnp.sum(acc[...], axis=1)

    sub = lax.broadcasted_iota(jnp.int32, (8, 128), 0)
    lane = lax.broadcasted_iota(jnp.int32, (8, 128), 1)

    def swap_bits(v, sub_bit, lane_bit):
        high, low = (sub >> sub_bit) & 1, (lane >> lane_bit) & 1
        rows_by, lanes_by = 1 << sub_bit, 1 << lane_bit
        from_high = pltpu.roll(pltpu.roll(v, 8 - rows_by, 0), lanes_by, 1)
        from_low = pltpu.roll(pltpu.roll(v, rows_by, 0), 128 - lanes_by, 1)
        return jnp.where(high == low, v, jnp.where(high == 0, from_high, from_low))

    strips = []
    for block in range(width // 128):
        v = whole[:, 128 * block : 128 * (block + 1)]
        for bit in range(3):
            v = swap_bits(v, bit, bit)
        for bit in range(3):
            v = swap_bits(v, bit, 3 + bit)
        strips += [v, pltpu.roll(v, 64, 1)]
    pieces = len(strips)
    for index in range(pieces):
        mine, above, below = strips[index], strips[(index + 1) % pieces], strips[index - 1]
        upper = pltpu.roll(jnp.where(sub == 0, above, mine), 7, 0)
        lower = pltpu.roll(jnp.where(sub == 7, below, mine), 1, 0)
        rim = jnp.where(lane < 32, upper, lower)
        packed = jnp.where(lane < 64, mine, pltpu.roll(rim, 64, 1))
        outgoing[8 * index : 8 * index + 8] = packed

    @pl.loop(0, SIDE_Z - 1)
    def _(order):
        by_z = SIDE_Z // 2 + order % 2 * -(order + 1) // 2 + (order + 1) % 2 * order // 2
        for spoke in spokes:
            send_tile(dict(by_z=by_z, **spoke)).start()

    for spoke in spokes:
        if any(spoke.values()):
            send_tile(spoke).start()
    incoming[pl.ds(group * count + me, 1)] = outgoing[pl.ds(me, 1)]

    for side in range(2):
        send_beside(side).wait_recv()
    rim_density = jnp.where(line < 4, beside[1, 0], beside[0, 0])
    rim_scale = jnp.where(line < 4, beside[1, 1], beside[0, 1])
    everyone = incoming.at[pl.ds(0, groups * count - 1)]
    pltpu.make_async_copy(everyone, everyone, tile_recv).wait()
    own_parts, rim_parts = [], []
    for index in range(0, pieces, 2):
        halves = []
        for half in (index, index + 1):
            v = incoming[8 * half : 8 * half + 8]
            for other in range(1, groups):
                v = v + incoming[other * count + 8 * half : other * count + 8 * half + 8]
            for bit in range(3):
                v = swap_bits(v, bit, 3 + bit)
            halves.append(v)
        own_parts.append(jnp.where(lane < 64, halves[0], pltpu.roll(halves[1], 64, 1)))
        rim_parts.append(jnp.where(lane < 64, pltpu.roll(halves[0], 64, 1), halves[1]))
    own = design[0] + design[1] * jnp.concatenate(own_parts, axis=1)
    rim = rim_density + rim_scale * jnp.concatenate(rim_parts, axis=1)
    sums = rings(own, jnp.where(rim_inside, rim, 0.0))
    filtered = jnp.zeros((8, width), jnp.float32)
    for place, key in enumerate(sorted(sums)):
        filtered = filtered + weights[place] * sums[key]
    base = math.tanh(sharpness * midpoint)
    projected[...] = (base + jnp.tanh(sharpness * (filtered - midpoint))) / (
        base + math.tanh(sharpness * (1.0 - midpoint))
    )
    for turn in range(STEPS):
        for run in range(2):
            send_p(run, turn).wait_send()
    for side in range(2):
        send_beside(side).wait_send()
    pltpu.make_async_copy(everyone, everyone, tile_send).wait()


def write_kernel(state, projected, forward_out, adjoint_out, projected_out, sems):
    copies = [
        pltpu.make_async_copy(state.at[run, comp], out.at[0, comp], sems.at[6 * run + comp])
        for run, out in enumerate((forward_out, adjoint_out))
        for comp in range(6)
    ]
    copies.append(pltpu.make_async_copy(projected, projected_out, sems.at[12]))
    for copy in copies:
        copy.start()
    for copy in copies:
        copy.wait()


def yee(*operands):
    forward = operands[1]
    density = operands[10]
    rows, high, wide = forward.shape[2:]
    plane = (rows, high, wide)
    width = density.shape[1]
    count = lax.axis_size("slab")
    groups = lax.axis_size("freq")
    operands = [
        operand if place == 7 else pltpu.with_memory_space_constraint(operand, pltpu.HBM)
        for place, operand in enumerate(operands)
    ]
    state, projected = pl.pallas_call(
        yee_kernel,
        out_shape=(
            pltpu.VMEM((2, 6) + plane, jnp.float32),
            pltpu.VMEM(density.shape, jnp.float32),
        ),
        in_specs=[pl.BlockSpec(memory_space=pl.ANY)] * 11,
        out_specs=[pl.BlockSpec(memory_space=pltpu.VMEM)] * 2,
        scratch_shapes=[
            pltpu.VMEM(plane, jnp.float32),
            pltpu.VMEM((2, 1, STEPS), jnp.float32),
            pltpu.VMEM((2, 1, wide), jnp.float32),
            pltpu.SMEM((2,), jnp.int32),
            pltpu.VMEM((2, high, wide), jnp.float32),
            pltpu.VMEM((STEPS, 2, 2, high, wide), jnp.float32),
            pltpu.VMEM((STEPS, 2, 2, high, wide), jnp.float32),
            pltpu.VMEM((STEPS, 2, 2, high, wide), jnp.float32),
            pltpu.VMEM((rows, 8, wide), jnp.float32),
            pltpu.VMEM(operands[8].shape, jnp.int32),
            pltpu.VMEM(operands[9].shape, jnp.int32),
            pltpu.VMEM((2, 8, width), jnp.float32),
            pltpu.VMEM((2, 2, 8, width), jnp.float32),
            pltpu.VMEM((15, 8, width), jnp.float32),
            pltpu.VMEM((count, 128), jnp.float32),
            pltpu.VMEM((groups * count, 128), jnp.float32),
            pltpu.SemaphoreType.DMA((5,)),
            pltpu.SemaphoreType.DMA((9,)),
            pltpu.SemaphoreType.DMA((STEPS, 2)),
            pltpu.SemaphoreType.DMA((STEPS, 2)),
            pltpu.SemaphoreType.DMA((STEPS, 2)),
            pltpu.SemaphoreType.DMA((STEPS, 2)),
            pltpu.SemaphoreType.REGULAR((4,)),
            pltpu.SemaphoreType.DMA((2,)),
            pltpu.SemaphoreType.DMA((2,)),
            pltpu.SemaphoreType.DMA,
            pltpu.SemaphoreType.DMA,
        ],
        compiler_params=pltpu.CompilerParams(
            collective_id=0, has_side_effects=True, vmem_limit_bytes=40 << 20
        ),
        name="yee",
    )(*operands)
    state = pltpu.with_memory_space_constraint(state, pltpu.VMEM)
    projected = pltpu.with_memory_space_constraint(projected, pltpu.VMEM)
    return pl.pallas_call(
        write_kernel,
        out_shape=(
            jax.ShapeDtypeStruct(forward.shape, jnp.float32),
            jax.ShapeDtypeStruct(forward.shape, jnp.float32),
            jax.ShapeDtypeStruct(density.shape, jnp.float32),
        ),
        in_specs=[pl.BlockSpec(memory_space=pltpu.VMEM)] * 2,
        out_specs=[pl.BlockSpec(memory_space=pl.ANY)] * 3,
        scratch_shapes=[pltpu.SemaphoreType.DMA((13,))],
        compiler_params=pltpu.CompilerParams(vmem_limit_bytes=8 << 20),
        name="write",
    )(state, projected)


def on_device(
    inverse_permittivity,
    forward_fields,
    adjoint_fields,
    source_wave,
    source_profile,
    adjoint_wave,
    adjoint_profile,
    source_plane,
    monitor_plane,
    radius_map,
    design_mask,
    design_density,
):
    return yee(
        inverse_permittivity,
        forward_fields,
        adjoint_fields,
        source_wave,
        source_profile,
        adjoint_wave,
        adjoint_profile,
        jnp.concatenate([source_plane, monitor_plane]),
        radius_map,
        design_mask,
        design_density,
    )


def solution(mesh):
    return jax.shard_map(
        on_device,
        mesh=mesh,
        in_specs=(
            P("slab", None, None),
            P("freq", None, "slab", None, None),
            P("freq", None, "slab", None, None),
            P("freq", None),
            P("freq", None),
            P("freq", None),
            P("freq", None),
            P("freq"),
            P("freq"),
            P("slab", None),
            P("slab", None),
            P("slab", None),
        ),
        out_specs=(
            P("freq", None, "slab", None, None),
            P("freq", None, "slab", None, None),
            P("slab", None),
        ),
        check_vma=False,
    )
```

```python
import math

import jax
import jax.numpy as jnp
from jax import lax
from jax.experimental import pallas as pl
from jax.experimental.pallas import tpu as pltpu
from jax.sharding import PartitionSpec as P

NY = 512
NZ = 24
FREQS = 4
STEPS = 3
RMAX = 4
SIDE_X, SIDE_Z, SIDE_Y = 4, 8, 2


courant = 0.5
sharpness = 4.0
midpoint = 0.5
step_size = 0.3


def next_y(v):
    lane = lax.broadcasted_iota(jnp.int32, v.shape, 1)
    return jnp.where(lane == v.shape[1] - 1, 0.0, pltpu.roll(v, v.shape[1] - 1, 1))


def prior_y(v):
    lane = lax.broadcasted_iota(jnp.int32, v.shape, 1)
    return jnp.where(lane == 0, 0.0, pltpu.roll(v, 1, 1))


def next_z(v):
    row = lax.broadcasted_iota(jnp.int32, v.shape, 0)
    return jnp.where(row == v.shape[0] - 1, 0.0, pltpu.roll(v, v.shape[0] - 1, 0))


def prior_z(v):
    row = lax.broadcasted_iota(jnp.int32, v.shape, 0)
    return jnp.where(row == 0, 0.0, pltpu.roll(v, 1, 0))


def swap_bits(v, sub_bit, lane_bit):
    sub = lax.broadcasted_iota(jnp.int32, (8, 128), 0)
    lane = lax.broadcasted_iota(jnp.int32, (8, 128), 1)
    high, low = (sub >> sub_bit) & 1, (lane >> lane_bit) & 1
    rows_by, lanes_by = 1 << sub_bit, 1 << lane_bit
    from_high = pltpu.roll(pltpu.roll(v, 8 - rows_by, 0), lanes_by, 1)
    from_low = pltpu.roll(pltpu.roll(v, rows_by, 0), 128 - lanes_by, 1)
    return jnp.where(high == low, v, jnp.where(high == 0, from_high, from_low))


def shift_x(v, by):
    if by == 0:
        return v
    width = v.shape[1]
    column = lax.broadcasted_iota(jnp.int32, v.shape, 1)
    inside = (column + by >= 0) & (column + by < width)
    return jnp.where(inside, pltpu.roll(v, (width - by) % width, 1), 0.0)


def shift_y(own, rim, by):
    if by == 0:
        return own
    line = lax.broadcasted_iota(jnp.int32, own.shape, 0)
    mixed = jnp.where(line < by, rim, own) if by > 0 else jnp.where(line >= 8 + by, rim, own)
    return pltpu.roll(mixed, (8 - by) % 8, 0)


def rings(own, rim):
    totals = {}
    for up in range(RMAX + 1):
        piece = shift_y(own, rim, up)
        if up:
            piece = piece + shift_y(own, rim, -up)
        for over in range(RMAX + 1):
            both = shift_x(piece, over)
            if over:
                both = both + shift_x(piece, -over)
            key = up * up + over * over
            totals[key] = totals[key] + both if key in totals else both
    return totals


def yee_kernel(
    inverse_hbm, forward_hbm, adjoint_hbm, swave_hbm, sprofile_hbm, awave_hbm, aprofile_hbm, planes_hbm,
    radius_hbm, mask_hbm, density_hbm,
    state, incoming, swapped, finish, weights,
    inverse, waves, profiles, planes, sources, partial, ghost_e, ghost_p, acc,
    radius, mask, beside, pairs, local, late, outgoing,
    load_sem, small_sem, e_send, e_recv, p_send, p_recv,
    greet_sem, beside_send, beside_recv, pair_send, pair_recv, tile_send, tile_recv, cross_send, cross_recv,
):
    count = lax.axis_size("slab")
    me = lax.axis_index("slab")
    right, left = lax.rem(me + 1, count), lax.rem(me + count - 1, count)
    is_last = me == count - 1
    is_first = me == 0
    rows = state.shape[2]
    top = rows - 1
    c = courant

    group = lax.axis_index("freq")
    groups = lax.axis_size("freq")
    at_x, at_line = lax.rem(me, SIDE_X), lax.div(me, SIDE_X)
    at_z, at_y = lax.rem(at_line, SIDE_Z), lax.div(at_line, SIDE_Z)
    at_far, at_core = lax.div(group, 2), lax.rem(group, 2)

    def turned(at, by, side):
        return lax.rem(at + by, side) if by else at

    def device(by_x=0, by_z=0, by_y=0, by_far=0, by_core=0):
        far, core = turned(at_far, by_far, 2), turned(at_core, by_core, 2)
        line = turned(at_y, by_y, SIDE_Y) * SIDE_Z + turned(at_z, by_z, SIDE_Z)
        return {"freq": far * 2 + core, "slab": line * SIDE_X + turned(at_x, by_x, SIDE_X)}

    line_x = [dict(by_x=by) for by in range(1, SIDE_X)]
    line_y = [
        dict(by_y=y, by_far=far, by_core=core)
        for y in range(2)
        for far in range(2)
        for core in range(2)
        if y + far + core
    ]
    near_z = [dict(by_z=1), dict(by_z=SIDE_Z - 1)]
    next_z_two = [dict(by_z=2), dict(by_z=SIDE_Z - 2)]
    rounds = [near_z, next_z_two, line_x, line_y]

    def signal(semaphore, partners):
        for partner in partners:
            pl.semaphore_signal(
                semaphore,
                inc=1,
                device_id=device(**partner),
                device_id_type=pl.DeviceIdType.MESH,
            )

    def greet(level):
        signal(greet_sem.at[level], rounds[level])

    def greeted(level):
        if level < len(rounds):
            pl.semaphore_wait(greet_sem.at[level], len(rounds[level]))
            if level + 1 < len(rounds):
                greet(level + 1)

    fields = (forward_hbm, adjoint_hbm)
    edges = [
        pltpu.make_async_copy(fields[run].at[0, :, top], state.at[run, :, top], load_sem.at[run])
        for run in range(2)
    ]
    loads = [
        pltpu.make_async_copy(
            fields[run].at[0, :, pl.ds(0, top)], state.at[run, :, pl.ds(0, top)], load_sem.at[2 + run]
        )
        for run in range(2)
    ]
    medium = pltpu.make_async_copy(inverse_hbm, inverse, load_sem.at[4])
    smalls = [
        pltpu.make_async_copy(swave_hbm, waves.at[0], small_sem.at[0]),
        pltpu.make_async_copy(awave_hbm, waves.at[1], small_sem.at[1]),
        pltpu.make_async_copy(sprofile_hbm, profiles.at[0], small_sem.at[2]),
        pltpu.make_async_copy(aprofile_hbm, profiles.at[1], small_sem.at[3]),
        pltpu.make_async_copy(planes_hbm, planes, small_sem.at[4]),
        pltpu.make_async_copy(radius_hbm, radius, small_sem.at[6]),
        pltpu.make_async_copy(mask_hbm, mask, small_sem.at[7]),
        pltpu.make_async_copy(density_hbm, finish.at[0], small_sem.at[8]),
    ]
    for copy in edges:
        copy.start()
    barrier = pltpu.get_barrier_semaphore()
    for neighbour in (left, right):
        pl.semaphore_signal(
            barrier, inc=1, device_id={"slab": neighbour}, device_id_type=pl.DeviceIdType.MESH
        )
    greetings = line_y + line_x + near_z
    signal(barrier, greetings)
    for copy in [loads[0], medium, loads[1]] + smalls:
        copy.start()

    def send_e(run, turn):
        return pltpu.make_async_remote_copy(
            src_ref=state.at[run, pl.ds(1, 2), 0] if turn else fields[run].at[0, pl.ds(1, 2), 0],
            dst_ref=ghost_e.at[turn, run],
            send_sem=e_send.at[turn, run],
            recv_sem=e_recv.at[turn, run],
            device_id={"slab": left},
            device_id_type=pl.DeviceIdType.MESH,
        )

    def send_p(run, turn):
        return pltpu.make_async_remote_copy(
            src_ref=partial.at[turn, run],
            dst_ref=ghost_p.at[turn, run],
            send_sem=p_send.at[turn, run],
            recv_sem=p_recv.at[turn, run],
            device_id={"slab": right},
            device_id_type=pl.DeviceIdType.MESH,
        )

    def make_partial(run, turn):
        elec_x, elec_y, elec_z = (state[run, comp, top] for comp in range(3))
        partial[turn, run, 0] = state[run, 4, top] - c * (next_z(elec_x) - elec_x + elec_z)
        partial[turn, run, 1] = state[run, 5, top] + c * (elec_y + next_y(elec_x) - elec_x)

    def magnetic_x(run, row):
        elec_y, elec_z = state[run, 1, row], state[run, 2, row]
        state[run, 3, row] = state[run, 3, row] - c * (
            next_y(elec_z) - elec_z - (next_z(elec_y) - elec_y)
        )

    def magnetic_row(run, row):
        magnetic_x(run, row)
        elec_x, elec_y, elec_z = (state[run, comp, row] for comp in range(3))
        state[run, 4, row] = state[run, 4, row] - c * (
            next_z(elec_x) - elec_x - (state[run, 2, row + 1] - elec_z)
        )
        state[run, 5, row] = state[run, 5, row] - c * (
            state[run, 1, row + 1] - elec_y - (next_y(elec_x) - elec_x)
        )

    def electric_row(run, row, turn, prior_hy, prior_hz):
        magn_x, magn_y, magn_z = (state[run, comp, row] for comp in range(3, 6))
        scaled = c * inverse[row]
        source = sources[run] * waves[run, :, turn : turn + 1]
        elec_x = (
            state[run, 0, row]
            + scaled * (magn_z - prior_y(magn_z) - (magn_y - prior_z(magn_y)))
            + source
        )
        elec_y = state[run, 1, row] + scaled * (magn_x - prior_z(magn_x) - (magn_z - prior_hz))
        elec_z = state[run, 2, row] + scaled * (magn_y - prior_hy - (magn_x - prior_y(magn_x)))
        state[run, 0, row] = elec_x
        state[run, 1, row] = elec_y
        state[run, 2, row] = elec_z
        if run == 1:
            total = (
                elec_x * state[0, 0, row] + elec_y * state[0, 1, row] + elec_z * state[0, 2, row]
            )
            folded = total[0:8] + total[8:16] + total[16:24]
            if turn == STEPS - 1 and isinstance(row, int):
                late[row // top] = jnp.sum(folded, axis=0)
            elif turn == 0:
                acc[row] = folded
            else:
                acc[row] = acc[row] + folded

    def interior(run, turn):
        magnetic_row(run, 0)

        @pl.loop(1, top)
        def _(row):
            magnetic_row(run, row)
            electric_row(run, row, turn, state[run, 4, row - 1], state[run, 5, row - 1])

        magnetic_x(run, top)

    def boundary(run, turn):
        send_e(run, turn).wait_recv()
        state[run, 4, top] = partial[turn, run, 0] + c * jnp.where(
            is_last, 0.0, ghost_e[turn, run, 1]
        )
        state[run, 5, top] = partial[turn, run, 1] - c * jnp.where(
            is_last, 0.0, ghost_e[turn, run, 0]
        )
        electric_row(run, top, turn, state[run, 4, top - 1], state[run, 5, top - 1])
        if turn < STEPS - 1:
            make_partial(run, turn + 1)
            send_p(run, turn + 1).start()
        send_p(run, turn).wait_recv()
        prior_hy = jnp.where(is_first, 0.0, ghost_p[turn, run, 0] + c * state[run, 2, 0])
        prior_hz = jnp.where(is_first, 0.0, ghost_p[turn, run, 1] - c * state[run, 1, 0])
        send_e(run, turn).wait_send()
        electric_row(run, 0, turn, prior_hy, prior_hz)
        if turn < STEPS - 1:
            send_e(run, turn + 1).start()

    def send_beside(side):
        return pltpu.make_async_remote_copy(
            src_ref=finish.at[pl.ds(0, 2)],
            dst_ref=beside.at[side],
            send_sem=beside_send.at[side],
            recv_sem=beside_recv.at[side],
            device_id={"slab": (right, left)[side]},
            device_id_type=pl.DeviceIdType.MESH,
        )

    crossed = at_core * 2 + at_far

    def send_tile(partner, sends, receives):
        there = device(**partner)["slab"]
        return pltpu.make_async_remote_copy(
            src_ref=outgoing.at[pl.ds(there, 1)],
            dst_ref=incoming.at[pl.ds(me, 1)],
            send_sem=sends,
            recv_sem=receives,
            device_id={"freq": crossed, "slab": there},
            device_id_type=pl.DeviceIdType.MESH,
        )

    def hops(by):
        far_x, far_z = min(by["by_x"], SIDE_X - by["by_x"]), min(by["by_z"], SIDE_Z - by["by_z"])
        return far_x + far_z + by["by_y"]

    spokes = sorted(
        (
            dict(by_x=x, by_z=z, by_y=y)
            for x in range(SIDE_X)
            for z in range(SIDE_Z)
            for y in range(SIDE_Y)
            if x + z + y
        ),
        key=hops,
        reverse=True,
    )

    def swap_cores(source, target, place):
        return pltpu.make_async_remote_copy(
            src_ref=source,
            dst_ref=target,
            send_sem=pair_send.at[place],
            recv_sem=pair_recv.at[place],
            device_id=device(by_core=1),
            device_id_type=pl.DeviceIdType.MESH,
        )

    pair = swap_cores(pairs.at[at_core], pairs.at[at_core], 0)

    edges[0].wait()
    make_partial(0, 0)
    pl.semaphore_wait(barrier, 2 + len(greetings))
    send_e(0, 0).start()
    send_p(0, 0).start()
    edges[1].wait()
    make_partial(1, 0)
    send_e(1, 0).start()
    send_p(1, 0).start()
    greet(0)
    for copy in smalls:
        copy.wait()
    for run in range(2):
        level = lax.broadcasted_iota(jnp.int32, sources.shape[1:], 0)
        hit = level == planes[run]
        sources[run] = jnp.where(hit, jnp.broadcast_to(profiles[run], hit.shape), 0.0)

    width = density_hbm.shape[1]
    scale = step_size / math.sqrt(3 * STEPS * NZ * FREQS)
    tile_x = width // radius.shape[1]
    column = lax.broadcasted_iota(jnp.int32, (8, width), 1)
    line = lax.broadcasted_iota(jnp.int32, (8, width), 0)

    def spread(table):
        wide = jnp.zeros((8, width), jnp.float32)
        for tile in range(table.shape[1]):
            value = jnp.broadcast_to(table[:, tile : tile + 1], (8, width)).astype(jnp.float32)
            wide = jnp.where(column // tile_x == tile, value, wide)
        return wide

    finish[1] = scale * spread(mask)
    reach = spread(radius)
    rim_inside = ((line < 4) & (me < count - 1)) | ((line >= 4) & (me > 0))

    def prepare_weights():
        counts = rings(jnp.ones((8, width), jnp.float32), jnp.where(rim_inside, 1.0, 0.0))
        total = jnp.zeros((8, width), jnp.float32)
        for key in counts:
            total = total + jnp.maximum(reach - math.sqrt(key), 0.0) * counts[key]
        for place, key in enumerate(sorted(counts)):
            weights[place] = jnp.maximum(reach - math.sqrt(key), 0.0) / total

    medium.wait()
    loads[0].wait()
    interior(0, 0)
    greeted(0)
    loads[1].wait()
    interior(1, 0)
    greeted(1)
    for turn in range(STEPS):
        for run in range(2):
            boundary(run, turn)
            if turn < STEPS - 1:
                interior(run, turn + 1)
            greeted(2 + 2 * turn + run)
        if turn == STEPS - 2:
            send_beside(0).start()
            send_beside(1).start()
            prepare_weights()
            local[...] = jnp.sum(acc[...], axis=1)

    ends = late[...]
    whole = local[...] + jnp.where(line == 0, ends[0:1], 0.0)
    pairs[at_core] = whole + jnp.where(line == top, ends[1:2], 0.0)
    pair.start()
    for side in range(2):
        send_beside(side).wait_recv()
    for place in range(2):
        rim = jnp.where(line < 4, beside[1, place], beside[0, place])
        finish[2 + place] = jnp.where(rim_inside, rim, 0.0)
    pair.wait_recv()
    whole = pairs[0] + pairs[1]
    sub = lax.broadcasted_iota(jnp.int32, (8, 128), 0)
    lane = lax.broadcasted_iota(jnp.int32, (8, 128), 1)
    strips = []
    for block in range(width // 128):
        v = whole[:, 128 * block : 128 * (block + 1)]
        for bit in range(3):
            v = swap_bits(v, bit, bit)
        for bit in range(3):
            v = swap_bits(v, bit, 3 + bit)
        strips += [v, pltpu.roll(v, 64, 1)]
    pieces = len(strips)
    for index in range(pieces):
        mine, above, below = strips[index], strips[(index + 1) % pieces], strips[index - 1]
        upper = pltpu.roll(jnp.where(sub == 0, above, mine), 7, 0)
        lower = pltpu.roll(jnp.where(sub == 7, below, mine), 1, 0)
        rim = jnp.where(lane < 32, upper, lower)
        packed = jnp.where(lane < 64, mine, pltpu.roll(rim, 64, 1))
        outgoing[8 * index : 8 * index + 8] = packed

    for spoke in spokes:
        send_tile(spoke, tile_send, tile_recv).start()

    @pl.when(at_far == at_core)
    def _():
        incoming[pl.ds(me, 1)] = outgoing[pl.ds(me, 1)]

    @pl.when(at_far != at_core)
    def _():
        cross = send_tile({}, cross_send, cross_recv)
        cross.start()
        cross.wait()

    everyone = incoming.at[pl.ds(0, len(spokes))]
    pltpu.make_async_copy(everyone, everyone, tile_recv).wait()
    swap = swap_cores(incoming, swapped, 1)
    swap.start()
    for turn in range(STEPS):
        for run in range(2):
            send_p(run, turn).wait_send()
    for side in range(2):
        send_beside(side).wait_send()
    pair.wait_send()
    pltpu.make_async_copy(everyone, everyone, tile_send).wait()
    swap.wait()


def write_kernel(
    state, incoming, swapped, finish, weights, forward_out, adjoint_out, projected_out, projected, sems
):
    copies = [
        pltpu.make_async_copy(state.at[run, comp], out.at[0, comp], sems.at[6 * run + comp])
        for run, out in enumerate((forward_out, adjoint_out))
        for comp in range(6)
    ]
    for copy in copies:
        copy.start()

    @pl.when(lax.axis_index("slab") >= 0)
    def _():
        lane = lax.broadcasted_iota(jnp.int32, (8, 128), 1)
        own_parts, rim_parts = [], []
        for index in range(0, incoming.shape[0] // 8, 2):
            halves = []
            for half in (index, index + 1):
                v = incoming[8 * half : 8 * half + 8] + swapped[8 * half : 8 * half + 8]
                for bit in range(3):
                    v = swap_bits(v, bit, 3 + bit)
                halves.append(v)
            own_parts.append(jnp.where(lane < 64, halves[0], pltpu.roll(halves[1], 64, 1)))
            rim_parts.append(jnp.where(lane < 64, pltpu.roll(halves[0], 64, 1), halves[1]))
        own = finish[0] + finish[1] * jnp.concatenate(own_parts, axis=1)
        rim = finish[2] + finish[3] * jnp.concatenate(rim_parts, axis=1)
        sums = rings(own, rim)
        filtered = jnp.zeros_like(own)
        for place, key in enumerate(sorted(sums)):
            filtered = filtered + weights[place] * sums[key]
        base = math.tanh(sharpness * midpoint)
        projected[...] = (base + jnp.tanh(sharpness * (filtered - midpoint))) / (
            base + math.tanh(sharpness * (1.0 - midpoint))
        )

    copies.append(pltpu.make_async_copy(projected, projected_out, sems.at[12]))
    copies[-1].start()
    for copy in copies:
        copy.wait()


def yee(*operands):
    forward = operands[1]
    density = operands[10]
    rows, high, wide = forward.shape[2:]
    plane = (rows, high, wide)
    width = density.shape[1]
    count = lax.axis_size("slab")
    groups = lax.axis_size("freq")
    operands = [
        operand if place == 7 else pltpu.with_memory_space_constraint(operand, pltpu.HBM)
        for place, operand in enumerate(operands)
    ]
    results = pl.pallas_call(
        yee_kernel,
        out_shape=(
            pltpu.VMEM((2, 6) + plane, jnp.float32),
            pltpu.VMEM((count, 128), jnp.float32),
            pltpu.VMEM((count, 128), jnp.float32),
            pltpu.VMEM((4, 8, width), jnp.float32),
            pltpu.VMEM((15, 8, width), jnp.float32),
        ),
        in_specs=[pl.BlockSpec(memory_space=pl.ANY)] * 11,
        out_specs=[pl.BlockSpec(memory_space=pltpu.VMEM)] * 5,
        scratch_shapes=[
            pltpu.VMEM(plane, jnp.float32),
            pltpu.VMEM((2, 1, STEPS), jnp.float32),
            pltpu.VMEM((2, 1, wide), jnp.float32),
            pltpu.SMEM((2,), jnp.int32),
            pltpu.VMEM((2, high, wide), jnp.float32),
            pltpu.VMEM((STEPS, 2, 2, high, wide), jnp.float32),
            pltpu.VMEM((STEPS, 2, 2, high, wide), jnp.float32),
            pltpu.VMEM((STEPS, 2, 2, high, wide), jnp.float32),
            pltpu.VMEM((rows, 8, wide), jnp.float32),
            pltpu.VMEM(operands[8].shape, jnp.int32),
            pltpu.VMEM(operands[9].shape, jnp.int32),
            pltpu.VMEM((2, 2, 8, width), jnp.float32),
            pltpu.VMEM((2, rows, wide), jnp.float32),
            pltpu.VMEM((rows, wide), jnp.float32),
            pltpu.VMEM((2, wide), jnp.float32),
            pltpu.VMEM((count, 128), jnp.float32),
            pltpu.SemaphoreType.DMA((5,)),
            pltpu.SemaphoreType.DMA((9,)),
            pltpu.SemaphoreType.DMA((STEPS, 2)),
            pltpu.SemaphoreType.DMA((STEPS, 2)),
            pltpu.SemaphoreType.DMA((STEPS, 2)),
            pltpu.SemaphoreType.DMA((STEPS, 2)),
            pltpu.SemaphoreType.REGULAR((4,)),
            pltpu.SemaphoreType.DMA((2,)),
            pltpu.SemaphoreType.DMA((2,)),
            pltpu.SemaphoreType.DMA((2,)),
            pltpu.SemaphoreType.DMA((2,)),
            pltpu.SemaphoreType.DMA,
            pltpu.SemaphoreType.DMA,
            pltpu.SemaphoreType.DMA,
            pltpu.SemaphoreType.DMA,
        ],
        compiler_params=pltpu.CompilerParams(
            collective_id=0, has_side_effects=True, vmem_limit_bytes=40 << 20
        ),
        name="yee",
    )(*operands)
    results = [pltpu.with_memory_space_constraint(result, pltpu.VMEM) for result in results]
    return pl.pallas_call(
        write_kernel,
        out_shape=(
            jax.ShapeDtypeStruct(forward.shape, jnp.float32),
            jax.ShapeDtypeStruct(forward.shape, jnp.float32),
            jax.ShapeDtypeStruct(density.shape, jnp.float32),
        ),
        in_specs=[pl.BlockSpec(memory_space=pltpu.VMEM)] * 5,
        out_specs=[pl.BlockSpec(memory_space=pl.ANY)] * 3,
        scratch_shapes=[pltpu.VMEM(density.shape, jnp.float32), pltpu.SemaphoreType.DMA((13,))],
        compiler_params=pltpu.CompilerParams(vmem_limit_bytes=8 << 20),
        name="write",
    )(*results)


def on_device(
    inverse_permittivity,
    forward_fields,
    adjoint_fields,
    source_wave,
    source_profile,
    adjoint_wave,
    adjoint_profile,
    source_plane,
    monitor_plane,
    radius_map,
    design_mask,
    design_density,
):
    return yee(
        inverse_permittivity,
        forward_fields,
        adjoint_fields,
        source_wave,
        source_profile,
        adjoint_wave,
        adjoint_profile,
        jnp.concatenate([source_plane, monitor_plane]),
        radius_map,
        design_mask,
        design_density,
    )


def solution(mesh):
    return jax.shard_map(
        on_device,
        mesh=mesh,
        in_specs=(
            P("slab", None, None),
            P("freq", None, "slab", None, None),
            P("freq", None, "slab", None, None),
            P("freq", None),
            P("freq", None),
            P("freq", None),
            P("freq", None),
            P("freq"),
            P("freq"),
            P("slab", None),
            P("slab", None),
            P("slab", None),
        ),
        out_specs=(
            P("freq", None, "slab", None, None),
            P("freq", None, "slab", None, None),
            P("slab", None),
        ),
        check_vma=False,
    )
```

```python
import math

import jax
import jax.numpy as jnp
from jax import lax
from jax.experimental import pallas as pl
from jax.experimental.pallas import tpu as pltpu
from jax.sharding import PartitionSpec as P

NY = 512
NZ = 24
FREQS = 4
STEPS = 3
RMAX = 4
SIDE_X, SIDE_Z, SIDE_Y = 4, 8, 2


courant = 0.5
sharpness = 4.0
midpoint = 0.5
step_size = 0.3


def next_y(v):
    lane = lax.broadcasted_iota(jnp.int32, v.shape, 1)
    return jnp.where(lane == v.shape[1] - 1, 0.0, pltpu.roll(v, v.shape[1] - 1, 1))


def prior_y(v):
    lane = lax.broadcasted_iota(jnp.int32, v.shape, 1)
    return jnp.where(lane == 0, 0.0, pltpu.roll(v, 1, 1))


def next_z(v):
    row = lax.broadcasted_iota(jnp.int32, v.shape, 0)
    return jnp.where(row == v.shape[0] - 1, 0.0, pltpu.roll(v, v.shape[0] - 1, 0))


def prior_z(v):
    row = lax.broadcasted_iota(jnp.int32, v.shape, 0)
    return jnp.where(row == 0, 0.0, pltpu.roll(v, 1, 0))


def swap_bits(v, sub_bit, lane_bit):
    sub = lax.broadcasted_iota(jnp.int32, (8, 128), 0)
    lane = lax.broadcasted_iota(jnp.int32, (8, 128), 1)
    high, low = (sub >> sub_bit) & 1, (lane >> lane_bit) & 1
    rows_by, lanes_by = 1 << sub_bit, 1 << lane_bit
    from_high = pltpu.roll(pltpu.roll(v, 8 - rows_by, 0), lanes_by, 1)
    from_low = pltpu.roll(pltpu.roll(v, rows_by, 0), 128 - lanes_by, 1)
    return jnp.where(high == low, v, jnp.where(high == 0, from_high, from_low))


def shift_x(v, by):
    if by == 0:
        return v
    width = v.shape[1]
    column = lax.broadcasted_iota(jnp.int32, v.shape, 1)
    inside = (column + by >= 0) & (column + by < width)
    return jnp.where(inside, pltpu.roll(v, (width - by) % width, 1), 0.0)


def shift_y(own, rim, by):
    if by == 0:
        return own
    line = lax.broadcasted_iota(jnp.int32, own.shape, 0)
    mixed = jnp.where(line < by, rim, own) if by > 0 else jnp.where(line >= 8 + by, rim, own)
    return pltpu.roll(mixed, (8 - by) % 8, 0)


def rings(own, rim):
    totals = {}
    for up in range(RMAX + 1):
        piece = shift_y(own, rim, up)
        if up:
            piece = piece + shift_y(own, rim, -up)
        for over in range(RMAX + 1):
            both = shift_x(piece, over)
            if over:
                both = both + shift_x(piece, -over)
            key = up * up + over * over
            totals[key] = totals[key] + both if key in totals else both
    return totals


def yee_kernel(
    inverse_hbm, forward_hbm, adjoint_hbm, swave_hbm, sprofile_hbm, awave_hbm, aprofile_hbm, planes_hbm,
    radius_hbm, mask_hbm, density_hbm,
    state, incoming, finish, weights,
    inverse, waves, profiles, planes, sources, partial, ghost_e, ghost_p, edge, soon, acc,
    radius, mask, beside, pairs, local, late, outgoing,
    load_sem, small_sem, e_send, e_recv, p_send, p_recv,
    greet_sem, beside_send, beside_recv, pair_send, pair_recv, tile_send, tile_recv,
):
    count = lax.axis_size("slab")
    me = lax.axis_index("slab")
    right, left = lax.rem(me + 1, count), lax.rem(me + count - 1, count)
    is_last = me == count - 1
    is_first = me == 0
    rows = state.shape[2]
    top = rows - 1
    c = courant

    group = lax.axis_index("freq")
    groups = lax.axis_size("freq")
    at_x, at_line = lax.rem(me, SIDE_X), lax.div(me, SIDE_X)
    at_z, at_y = lax.rem(at_line, SIDE_Z), lax.div(at_line, SIDE_Z)
    at_far, at_core = lax.div(group, 2), lax.rem(group, 2)

    def turned(at, by, side):
        return lax.rem(at + by, side) if by else at

    def device(by_x=0, by_z=0, by_y=0, by_far=0, by_core=0):
        far, core = turned(at_far, by_far, 2), turned(at_core, by_core, 2)
        line = turned(at_y, by_y, SIDE_Y) * SIDE_Z + turned(at_z, by_z, SIDE_Z)
        return {"freq": far * 2 + core, "slab": line * SIDE_X + turned(at_x, by_x, SIDE_X)}

    line_x = [dict(by_x=by) for by in range(1, SIDE_X)]
    line_y = [
        dict(by_y=y, by_far=far, by_core=core)
        for y in range(2)
        for far in range(2)
        for core in range(2)
        if y + far + core
    ]
    near_z = [dict(by_z=1), dict(by_z=SIDE_Z - 1)]
    next_z_two = [dict(by_z=2), dict(by_z=SIDE_Z - 2)]
    rounds = [near_z, next_z_two, line_x, line_y]

    def signal(semaphore, partners):
        for partner in partners:
            pl.semaphore_signal(
                semaphore,
                inc=1,
                device_id=device(**partner),
                device_id_type=pl.DeviceIdType.MESH,
            )

    def greet(level):
        signal(greet_sem.at[level], rounds[level])

    def greeted(level):
        if level < len(rounds):
            pl.semaphore_wait(greet_sem.at[level], len(rounds[level]))
            if level + 1 < len(rounds):
                greet(level + 1)

    fields = (forward_hbm, adjoint_hbm)
    edges = [
        pltpu.make_async_copy(fields[run].at[0, :, top], state.at[run, :, top], load_sem.at[run])
        for run in range(2)
    ]
    loads = [
        pltpu.make_async_copy(
            fields[run].at[0, :, pl.ds(0, top)], state.at[run, :, pl.ds(0, top)], load_sem.at[2 + run]
        )
        for run in range(2)
    ]
    medium = pltpu.make_async_copy(inverse_hbm, inverse, load_sem.at[4])
    smalls = [
        pltpu.make_async_copy(swave_hbm, waves.at[0], small_sem.at[0]),
        pltpu.make_async_copy(awave_hbm, waves.at[1], small_sem.at[1]),
        pltpu.make_async_copy(sprofile_hbm, profiles.at[0], small_sem.at[2]),
        pltpu.make_async_copy(aprofile_hbm, profiles.at[1], small_sem.at[3]),
        pltpu.make_async_copy(planes_hbm, planes, small_sem.at[4]),
        pltpu.make_async_copy(radius_hbm, radius, small_sem.at[6]),
        pltpu.make_async_copy(mask_hbm, mask, small_sem.at[7]),
        pltpu.make_async_copy(density_hbm, finish.at[0], small_sem.at[8]),
    ]
    for copy in edges:
        copy.start()
    barrier = pltpu.get_barrier_semaphore()
    for neighbour in (left, right):
        pl.semaphore_signal(
            barrier, inc=1, device_id={"slab": neighbour}, device_id_type=pl.DeviceIdType.MESH
        )
    greetings = line_y + line_x + near_z
    signal(barrier, greetings)
    for copy in [loads[0], medium, loads[1]] + smalls:
        copy.start()

    def send_e(run, turn):
        return pltpu.make_async_remote_copy(
            src_ref=edge.at[turn - 1, run] if turn else fields[run].at[0, pl.ds(1, 2), 0],
            dst_ref=ghost_e.at[turn, run],
            send_sem=e_send.at[turn, run],
            recv_sem=e_recv.at[turn, run],
            device_id={"slab": left},
            device_id_type=pl.DeviceIdType.MESH,
        )

    def send_p(run, turn):
        return pltpu.make_async_remote_copy(
            src_ref=partial.at[turn, run],
            dst_ref=ghost_p.at[turn, run],
            send_sem=p_send.at[turn, run],
            recv_sem=p_recv.at[turn, run],
            device_id={"slab": right},
            device_id_type=pl.DeviceIdType.MESH,
        )

    def make_partial(run, turn):
        elec_x, elec_y, elec_z = (state[run, comp, top] for comp in range(3))
        partial[turn, run, 0] = state[run, 4, top] - c * (next_z(elec_x) - elec_x + elec_z)
        partial[turn, run, 1] = state[run, 5, top] + c * (elec_y + next_y(elec_x) - elec_x)

    def magnetic_x(run, row):
        elec_y, elec_z = state[run, 1, row], state[run, 2, row]
        state[run, 3, row] = state[run, 3, row] - c * (
            next_y(elec_z) - elec_z - (next_z(elec_y) - elec_y)
        )

    def magnetic_row(run, row):
        magnetic_x(run, row)
        elec_x, elec_y, elec_z = (state[run, comp, row] for comp in range(3))
        state[run, 4, row] = state[run, 4, row] - c * (
            next_z(elec_x) - elec_x - (state[run, 2, row + 1] - elec_z)
        )
        state[run, 5, row] = state[run, 5, row] - c * (
            state[run, 1, row + 1] - elec_y - (next_y(elec_x) - elec_x)
        )

    def keep(row, turn, elec_x, elec_y, elec_z):
        total = elec_x * state[0, 0, row] + elec_y * state[0, 1, row] + elec_z * state[0, 2, row]
        folded = total[0:8] + total[8:16] + total[16:24]
        if turn == STEPS - 1 and isinstance(row, int):
            late[row // top] = jnp.sum(folded, axis=0)
        elif turn == 0:
            acc[row] = folded
        else:
            acc[row] = acc[row] + folded

    def electric_row(run, row, turn, prior_hy, prior_hz):
        magn_x, magn_y, magn_z = (state[run, comp, row] for comp in range(3, 6))
        scaled = c * inverse[row]
        source = sources[run] * waves[run, :, turn : turn + 1]
        elec_x = (
            state[run, 0, row]
            + scaled * (magn_z - prior_y(magn_z) - (magn_y - prior_z(magn_y)))
            + source
        )
        elec_y = state[run, 1, row] + scaled * (magn_x - prior_z(magn_x) - (magn_z - prior_hz))
        elec_z = state[run, 2, row] + scaled * (magn_y - prior_hy - (magn_x - prior_y(magn_x)))
        state[run, 0, row] = elec_x
        state[run, 1, row] = elec_y
        state[run, 2, row] = elec_z
        if run == 1:
            keep(row, turn, elec_x, elec_y, elec_z)

    def interior(run, turn):
        magnetic_row(run, 0)

        @pl.loop(1, top)
        def _(row):
            magnetic_row(run, row)
            electric_row(run, row, turn, state[run, 4, row - 1], state[run, 5, row - 1])

        magnetic_x(run, top)
        ready(run, turn)

    def ready(run, turn):
        magn_x, magn_y, magn_z = (state[run, comp, 0] for comp in range(3, 6))
        scaled = c * inverse[0]
        reached = jnp.where(is_first, 0.0, scaled)
        source = sources[run] * waves[run, :, turn : turn + 1]
        elec_y, elec_z = state[run, 1, 0], state[run, 2, 0]
        soon[run, 5] = (
            state[run, 0, 0]
            + scaled * (magn_z - prior_y(magn_z) - (magn_y - prior_z(magn_y)))
            + source
        )
        soon[run, 0] = (
            elec_y + scaled * (magn_x - prior_z(magn_x) - magn_z) - reached * (c * elec_y)
        )
        soon[run, 1] = (
            elec_z + scaled * (magn_y - (magn_x - prior_y(magn_x))) - reached * (c * elec_z)
        )
        magn_x = state[run, 3, top]
        scaled = c * inverse[top]
        soon[run, 2] = state[run, 0, top] + source
        soon[run, 3] = state[run, 1, top] + scaled * (
            magn_x - prior_z(magn_x) + state[run, 5, top - 1]
        )
        soon[run, 4] = state[run, 2, top] - scaled * (
            magn_x - prior_y(magn_x) + state[run, 4, top - 1]
        )

    def boundary(run, turn):
        send_p(run, turn).wait_recv()
        reached = jnp.where(is_first, 0.0, c * inverse[0])
        elec_y = soon[run, 0] + reached * ghost_p[turn, run, 1]
        elec_z = soon[run, 1] - reached * ghost_p[turn, run, 0]
        if turn < STEPS - 1:
            edge[turn, run, 0] = elec_y
            edge[turn, run, 1] = elec_z
            send_e(run, turn + 1).start()
        else:
            state[run, 1, 0] = elec_y
            state[run, 2, 0] = elec_z
        send_e(run, turn).wait_recv()
        state[run, 0, 0] = soon[run, 5]
        if turn < STEPS - 1:
            state[run, 1, 0] = elec_y
            state[run, 2, 0] = elec_z
        scaled = c * inverse[top]
        magn_y = partial[turn, run, 0] + c * jnp.where(is_last, 0.0, ghost_e[turn, run, 1])
        magn_z = partial[turn, run, 1] - c * jnp.where(is_last, 0.0, ghost_e[turn, run, 0])
        elec_x = soon[run, 2] + scaled * (
            magn_z - prior_y(magn_z) - (magn_y - prior_z(magn_y))
        )
        elec_y = soon[run, 3] - scaled * magn_z
        elec_z = soon[run, 4] + scaled * magn_y
        if turn < STEPS - 1:
            partial[turn + 1, run, 0] = magn_y - c * (next_z(elec_x) - elec_x + elec_z)
            partial[turn + 1, run, 1] = magn_z + c * (elec_y + next_y(elec_x) - elec_x)
            send_p(run, turn + 1).start()
        state[run, 4, top] = magn_y
        state[run, 5, top] = magn_z
        state[run, 0, top] = elec_x
        state[run, 1, top] = elec_y
        state[run, 2, top] = elec_z
        if run == 1:
            for row in (0, top):
                keep(row, turn, *(state[1, comp, row] for comp in range(3)))

    def send_beside(side):
        return pltpu.make_async_remote_copy(
            src_ref=finish.at[pl.ds(0, 2)],
            dst_ref=beside.at[side],
            send_sem=beside_send.at[side],
            recv_sem=beside_recv.at[side],
            device_id={"slab": (right, left)[side]},
            device_id_type=pl.DeviceIdType.MESH,
        )

    def send_tile(partner):
        there = device(**partner)
        return pltpu.make_async_remote_copy(
            src_ref=outgoing.at[pl.ds(there["slab"], 1)],
            dst_ref=incoming.at[pl.ds(at_far * count + me, 1)],
            send_sem=tile_send,
            recv_sem=tile_recv,
            device_id=there,
            device_id_type=pl.DeviceIdType.MESH,
        )

    def hops(by):
        far_x, far_z = min(by["by_x"], SIDE_X - by["by_x"]), min(by["by_z"], SIDE_Z - by["by_z"])
        return far_x + far_z + (1 if by["by_y"] else 2 * by["by_far"])

    spokes = sorted(
        (
            dict(by_x=x, by_z=z, by_y=y, by_far=far)
            for x in range(SIDE_X)
            for z in range(SIDE_Z)
            for y in range(SIDE_Y)
            for far in range(2)
            if x + z + y + far
        ),
        key=hops,
        reverse=True,
    )

    def swap_cores(source, target):
        return pltpu.make_async_remote_copy(
            src_ref=source,
            dst_ref=target,
            send_sem=pair_send,
            recv_sem=pair_recv,
            device_id=device(by_core=1),
            device_id_type=pl.DeviceIdType.MESH,
        )

    pair = swap_cores(pairs.at[at_core], pairs.at[at_core])

    edges[0].wait()
    make_partial(0, 0)
    pl.semaphore_wait(barrier, 2 + len(greetings))
    send_e(0, 0).start()
    send_p(0, 0).start()
    edges[1].wait()
    make_partial(1, 0)
    send_e(1, 0).start()
    send_p(1, 0).start()
    greet(0)
    for copy in smalls:
        copy.wait()
    for run in range(2):
        level = lax.broadcasted_iota(jnp.int32, sources.shape[1:], 0)
        hit = level == planes[run]
        sources[run] = jnp.where(hit, jnp.broadcast_to(profiles[run], hit.shape), 0.0)

    width = density_hbm.shape[1]
    scale = step_size / math.sqrt(3 * STEPS * NZ * FREQS)
    tile_x = width // radius.shape[1]
    column = lax.broadcasted_iota(jnp.int32, (8, width), 1)
    line = lax.broadcasted_iota(jnp.int32, (8, width), 0)

    def spread(table):
        wide = jnp.zeros((8, width), jnp.float32)
        for tile in range(table.shape[1]):
            value = jnp.broadcast_to(table[:, tile : tile + 1], (8, width)).astype(jnp.float32)
            wide = jnp.where(column // tile_x == tile, value, wide)
        return wide

    finish[1] = scale * spread(mask)
    reach = spread(radius)
    rim_inside = ((line < 4) & (me < count - 1)) | ((line >= 4) & (me > 0))

    def prepare_weights():
        counts = rings(jnp.ones((8, width), jnp.float32), jnp.where(rim_inside, 1.0, 0.0))
        total = jnp.zeros((8, width), jnp.float32)
        for key in counts:
            total = total + jnp.maximum(reach - math.sqrt(key), 0.0) * counts[key]
        for place, key in enumerate(sorted(counts)):
            weights[place] = jnp.maximum(reach - math.sqrt(key), 0.0) / total

    medium.wait()
    loads[0].wait()
    interior(0, 0)
    greeted(0)
    loads[1].wait()
    interior(1, 0)
    greeted(1)
    for turn in range(STEPS):
        for run in range(2):
            boundary(run, turn)
            if turn < STEPS - 1:
                interior(run, turn + 1)
            greeted(2 + 2 * turn + run)
        if turn == STEPS - 2:
            send_beside(0).start()
            send_beside(1).start()
            prepare_weights()
            local[...] = jnp.sum(acc[...], axis=1)

    ends = late[...]
    whole = local[...] + jnp.where(line == 0, ends[0:1], 0.0)
    pairs[at_core] = whole + jnp.where(line == top, ends[1:2], 0.0)
    pair.start()
    for side in range(2):
        send_beside(side).wait_recv()
    for place in range(2):
        rim = jnp.where(line < 4, beside[1, place], beside[0, place])
        finish[2 + place] = jnp.where(rim_inside, rim, 0.0)
    pair.wait_recv()
    whole = pairs[0] + pairs[1]
    sub = lax.broadcasted_iota(jnp.int32, (8, 128), 0)
    lane = lax.broadcasted_iota(jnp.int32, (8, 128), 1)
    strips = []
    for block in range(width // 128):
        v = whole[:, 128 * block : 128 * (block + 1)]
        for bit in range(3):
            v = swap_bits(v, bit, bit)
        for bit in range(3):
            v = swap_bits(v, bit, 3 + bit)
        strips += [v, pltpu.roll(v, 64, 1)]
    pieces = len(strips)
    for index in range(pieces):
        mine, above, below = strips[index], strips[(index + 1) % pieces], strips[index - 1]
        upper = pltpu.roll(jnp.where(sub == 0, above, mine), 7, 0)
        lower = pltpu.roll(jnp.where(sub == 7, below, mine), 1, 0)
        rim = jnp.where(lane < 32, upper, lower)
        packed = jnp.where(lane < 64, mine, pltpu.roll(rim, 64, 1))
        outgoing[8 * index : 8 * index + 8] = packed

    for spoke in spokes:
        send_tile(spoke).start()
    incoming[pl.ds(at_far * count + me, 1)] = outgoing[pl.ds(me, 1)]
    everyone = incoming.at[pl.ds(0, len(spokes))]
    pltpu.make_async_copy(everyone, everyone, tile_recv).wait()
    for turn in range(STEPS):
        for run in range(2):
            send_e(run, turn).wait_send()
            send_p(run, turn).wait_send()
    for side in range(2):
        send_beside(side).wait_send()
    pair.wait_send()
    pltpu.make_async_copy(everyone, everyone, tile_send).wait()


def write_kernel(
    state, incoming, finish, weights, forward_out, adjoint_out, projected_out, projected, sems
):
    copies = [
        pltpu.make_async_copy(state.at[run, comp], out.at[0, comp], sems.at[6 * run + comp])
        for run, out in enumerate((forward_out, adjoint_out))
        for comp in range(6)
    ]
    for copy in copies:
        copy.start()

    @pl.when(lax.axis_index("slab") >= 0)
    def _():
        lane = lax.broadcasted_iota(jnp.int32, (8, 128), 1)
        own_parts, rim_parts = [], []
        count = incoming.shape[0] // 2
        for index in range(0, count // 8, 2):
            halves = []
            for half in (index, index + 1):
                v = incoming[8 * half : 8 * half + 8] + incoming[count + 8 * half : count + 8 * half + 8]
                for bit in range(3):
                    v = swap_bits(v, bit, 3 + bit)
                halves.append(v)
            own_parts.append(jnp.where(lane < 64, halves[0], pltpu.roll(halves[1], 64, 1)))
            rim_parts.append(jnp.where(lane < 64, pltpu.roll(halves[0], 64, 1), halves[1]))
        own = finish[0] + finish[1] * jnp.concatenate(own_parts, axis=1)
        rim = finish[2] + finish[3] * jnp.concatenate(rim_parts, axis=1)
        sums = rings(own, rim)
        filtered = jnp.zeros_like(own)
        for place, key in enumerate(sorted(sums)):
            filtered = filtered + weights[place] * sums[key]
        base = math.tanh(sharpness * midpoint)
        projected[...] = (base + jnp.tanh(sharpness * (filtered - midpoint))) / (
            base + math.tanh(sharpness * (1.0 - midpoint))
        )

    copies.append(pltpu.make_async_copy(projected, projected_out, sems.at[12]))
    copies[-1].start()
    for copy in copies:
        copy.wait()


def yee(*operands):
    forward = operands[1]
    density = operands[10]
    rows, high, wide = forward.shape[2:]
    plane = (rows, high, wide)
    width = density.shape[1]
    count = lax.axis_size("slab")
    groups = lax.axis_size("freq")
    operands = [
        operand if place == 7 else pltpu.with_memory_space_constraint(operand, pltpu.HBM)
        for place, operand in enumerate(operands)
    ]
    results = pl.pallas_call(
        yee_kernel,
        out_shape=(
            pltpu.VMEM((2, 6) + plane, jnp.float32),
            pltpu.VMEM((2 * count, 128), jnp.float32),
            pltpu.VMEM((4, 8, width), jnp.float32),
            pltpu.VMEM((15, 8, width), jnp.float32),
        ),
        in_specs=[pl.BlockSpec(memory_space=pl.ANY)] * 11,
        out_specs=[pl.BlockSpec(memory_space=pltpu.VMEM)] * 4,
        scratch_shapes=[
            pltpu.VMEM(plane, jnp.float32),
            pltpu.VMEM((2, 1, STEPS), jnp.float32),
            pltpu.VMEM((2, 1, wide), jnp.float32),
            pltpu.SMEM((2,), jnp.int32),
            pltpu.VMEM((2, high, wide), jnp.float32),
            pltpu.VMEM((STEPS, 2, 2, high, wide), jnp.float32),
            pltpu.VMEM((STEPS, 2, 2, high, wide), jnp.float32),
            pltpu.VMEM((STEPS, 2, 2, high, wide), jnp.float32),
            pltpu.VMEM((STEPS - 1, 2, 2, high, wide), jnp.float32),
            pltpu.VMEM((2, 6, high, wide), jnp.float32),
            pltpu.VMEM((rows, 8, wide), jnp.float32),
            pltpu.VMEM(operands[8].shape, jnp.int32),
            pltpu.VMEM(operands[9].shape, jnp.int32),
            pltpu.VMEM((2, 2, 8, width), jnp.float32),
            pltpu.VMEM((2, rows, wide), jnp.float32),
            pltpu.VMEM((rows, wide), jnp.float32),
            pltpu.VMEM((2, wide), jnp.float32),
            pltpu.VMEM((count, 128), jnp.float32),
            pltpu.SemaphoreType.DMA((5,)),
            pltpu.SemaphoreType.DMA((9,)),
            pltpu.SemaphoreType.DMA((STEPS, 2)),
            pltpu.SemaphoreType.DMA((STEPS, 2)),
            pltpu.SemaphoreType.DMA((STEPS, 2)),
            pltpu.SemaphoreType.DMA((STEPS, 2)),
            pltpu.SemaphoreType.REGULAR((4,)),
            pltpu.SemaphoreType.DMA((2,)),
            pltpu.SemaphoreType.DMA((2,)),
            pltpu.SemaphoreType.DMA,
            pltpu.SemaphoreType.DMA,
            pltpu.SemaphoreType.DMA,
            pltpu.SemaphoreType.DMA,
        ],
        compiler_params=pltpu.CompilerParams(
            collective_id=0, has_side_effects=True, vmem_limit_bytes=40 << 20
        ),
        name="yee",
    )(*operands)
    results = [pltpu.with_memory_space_constraint(result, pltpu.VMEM) for result in results]
    return pl.pallas_call(
        write_kernel,
        out_shape=(
            jax.ShapeDtypeStruct(forward.shape, jnp.float32),
            jax.ShapeDtypeStruct(forward.shape, jnp.float32),
            jax.ShapeDtypeStruct(density.shape, jnp.float32),
        ),
        in_specs=[pl.BlockSpec(memory_space=pltpu.VMEM)] * 4,
        out_specs=[pl.BlockSpec(memory_space=pl.ANY)] * 3,
        scratch_shapes=[pltpu.VMEM(density.shape, jnp.float32), pltpu.SemaphoreType.DMA((13,))],
        compiler_params=pltpu.CompilerParams(vmem_limit_bytes=8 << 20),
        name="write",
    )(*results)


def on_device(
    inverse_permittivity,
    forward_fields,
    adjoint_fields,
    source_wave,
    source_profile,
    adjoint_wave,
    adjoint_profile,
    source_plane,
    monitor_plane,
    radius_map,
    design_mask,
    design_density,
):
    return yee(
        inverse_permittivity,
        forward_fields,
        adjoint_fields,
        source_wave,
        source_profile,
        adjoint_wave,
        adjoint_profile,
        jnp.concatenate([source_plane, monitor_plane]),
        radius_map,
        design_mask,
        design_density,
    )


def solution(mesh):
    return jax.shard_map(
        on_device,
        mesh=mesh,
        in_specs=(
            P("slab", None, None),
            P("freq", None, "slab", None, None),
            P("freq", None, "slab", None, None),
            P("freq", None),
            P("freq", None),
            P("freq", None),
            P("freq", None),
            P("freq"),
            P("freq"),
            P("slab", None),
            P("slab", None),
            P("slab", None),
        ),
        out_specs=(
            P("freq", None, "slab", None, None),
            P("freq", None, "slab", None, None),
            P("slab", None),
        ),
        check_vma=False,
    )
```

```python
import math

import jax
import jax.numpy as jnp
from jax import lax
from jax.experimental import pallas as pl
from jax.experimental.pallas import tpu as pltpu
from jax.sharding import PartitionSpec as P

NY = 512
NZ = 24
FREQS = 4
STEPS = 3
RMAX = 4
SIDE_X, SIDE_Z, SIDE_Y = 4, 8, 2


courant = 0.5
sharpness = 4.0
midpoint = 0.5
step_size = 0.3


def next_y(v):
    lane = lax.broadcasted_iota(jnp.int32, v.shape, 1)
    return jnp.where(lane == v.shape[1] - 1, 0.0, pltpu.roll(v, v.shape[1] - 1, 1))


def prior_y(v):
    lane = lax.broadcasted_iota(jnp.int32, v.shape, 1)
    return jnp.where(lane == 0, 0.0, pltpu.roll(v, 1, 1))


def next_z(v):
    row = lax.broadcasted_iota(jnp.int32, v.shape, 0)
    return jnp.where(row == v.shape[0] - 1, 0.0, pltpu.roll(v, v.shape[0] - 1, 0))


def prior_z(v):
    row = lax.broadcasted_iota(jnp.int32, v.shape, 0)
    return jnp.where(row == 0, 0.0, pltpu.roll(v, 1, 0))


def swap_bits(v, sub_bit, lane_bit):
    sub = lax.broadcasted_iota(jnp.int32, (8, 128), 0)
    lane = lax.broadcasted_iota(jnp.int32, (8, 128), 1)
    high, low = (sub >> sub_bit) & 1, (lane >> lane_bit) & 1
    rows_by, lanes_by = 1 << sub_bit, 1 << lane_bit
    from_high = pltpu.roll(pltpu.roll(v, 8 - rows_by, 0), lanes_by, 1)
    from_low = pltpu.roll(pltpu.roll(v, rows_by, 0), 128 - lanes_by, 1)
    return jnp.where(high == low, v, jnp.where(high == 0, from_high, from_low))


def shift_x(v, by):
    if by == 0:
        return v
    width = v.shape[1]
    column = lax.broadcasted_iota(jnp.int32, v.shape, 1)
    inside = (column + by >= 0) & (column + by < width)
    return jnp.where(inside, pltpu.roll(v, (width - by) % width, 1), 0.0)


def shift_y(own, rim, by):
    if by == 0:
        return own
    line = lax.broadcasted_iota(jnp.int32, own.shape, 0)
    mixed = jnp.where(line < by, rim, own) if by > 0 else jnp.where(line >= 8 + by, rim, own)
    return pltpu.roll(mixed, (8 - by) % 8, 0)


def rings(own, rim):
    totals = {}
    for up in range(RMAX + 1):
        piece = shift_y(own, rim, up)
        if up:
            piece = piece + shift_y(own, rim, -up)
        for over in range(RMAX + 1):
            both = shift_x(piece, over)
            if over:
                both = both + shift_x(piece, -over)
            key = up * up + over * over
            totals[key] = totals[key] + both if key in totals else both
    return totals


def yee_kernel(
    inverse_hbm, forward_hbm, adjoint_hbm, swave_hbm, sprofile_hbm, awave_hbm, aprofile_hbm, planes_hbm,
    radius_hbm, mask_hbm, density_hbm,
    state, incoming, finish, weights,
    inverse, waves, profiles, planes, sources, partial, ghost_e, ghost_p, edge, soon, acc,
    radius, mask, beside, pairs, local, late, outgoing,
    load_sem, small_sem, e_send, e_recv, p_send, p_recv,
    greet_sem, beside_send, beside_recv, pair_send, pair_recv, tile_send, tile_recv,
):
    count = lax.axis_size("slab")
    me = lax.axis_index("slab")
    right, left = lax.rem(me + 1, count), lax.rem(me + count - 1, count)
    is_last = me == count - 1
    is_first = me == 0
    rows = state.shape[2]
    top = rows - 1
    c = courant

    group = lax.axis_index("freq")
    groups = lax.axis_size("freq")
    at_x, at_line = lax.rem(me, SIDE_X), lax.div(me, SIDE_X)
    at_z, at_y = lax.rem(at_line, SIDE_Z), lax.div(at_line, SIDE_Z)
    at_far, at_core = lax.div(group, 2), lax.rem(group, 2)

    def turned(at, by, side):
        return lax.rem(at + by, side) if by else at

    def device(by_x=0, by_z=0, by_y=0, by_far=0, by_core=0):
        far, core = turned(at_far, by_far, 2), turned(at_core, by_core, 2)
        line = turned(at_y, by_y, SIDE_Y) * SIDE_Z + turned(at_z, by_z, SIDE_Z)
        return {"freq": far * 2 + core, "slab": line * SIDE_X + turned(at_x, by_x, SIDE_X)}

    line_x = [dict(by_x=by) for by in range(1, SIDE_X)]
    line_y = [
        dict(by_y=y, by_far=far, by_core=core)
        for y in range(2)
        for far in range(2)
        for core in range(2)
        if y + far + core
    ]
    near_z = [dict(by_z=1), dict(by_z=SIDE_Z - 1)]
    next_z_two = [dict(by_z=2), dict(by_z=SIDE_Z - 2)]
    rounds = [near_z, next_z_two, line_x, line_y]

    def signal(semaphore, partners):
        for partner in partners:
            pl.semaphore_signal(
                semaphore,
                inc=1,
                device_id=device(**partner),
                device_id_type=pl.DeviceIdType.MESH,
            )

    def greet(level):
        signal(greet_sem.at[level], rounds[level])

    def greeted(level):
        if level < len(rounds):
            pl.semaphore_wait(greet_sem.at[level], len(rounds[level]))
            if level + 1 < len(rounds):
                greet(level + 1)

    fields = (forward_hbm, adjoint_hbm)
    edges = [
        pltpu.make_async_copy(fields[run].at[0, :, top], state.at[run, :, top], load_sem.at[run])
        for run in range(2)
    ]
    loads = [
        pltpu.make_async_copy(
            fields[run].at[0, :, pl.ds(0, top)], state.at[run, :, pl.ds(0, top)], load_sem.at[2 + run]
        )
        for run in range(2)
    ]
    medium = pltpu.make_async_copy(inverse_hbm, inverse, load_sem.at[4])
    smalls = [
        pltpu.make_async_copy(swave_hbm, waves.at[0], small_sem.at[0]),
        pltpu.make_async_copy(awave_hbm, waves.at[1], small_sem.at[1]),
        pltpu.make_async_copy(sprofile_hbm, profiles.at[0], small_sem.at[2]),
        pltpu.make_async_copy(aprofile_hbm, profiles.at[1], small_sem.at[3]),
        pltpu.make_async_copy(planes_hbm, planes, small_sem.at[4]),
        pltpu.make_async_copy(radius_hbm, radius, small_sem.at[6]),
        pltpu.make_async_copy(mask_hbm, mask, small_sem.at[7]),
        pltpu.make_async_copy(density_hbm, finish.at[0], small_sem.at[8]),
    ]
    for copy in edges:
        copy.start()
    barrier = pltpu.get_barrier_semaphore()
    for neighbour in (left, right):
        pl.semaphore_signal(
            barrier, inc=1, device_id={"slab": neighbour}, device_id_type=pl.DeviceIdType.MESH
        )
    greetings = line_y + line_x + near_z
    signal(barrier, greetings)
    for copy in [loads[0], medium, loads[1]] + smalls:
        copy.start()

    def send_e(run, turn):
        return pltpu.make_async_remote_copy(
            src_ref=edge.at[turn - 1, run] if turn else fields[run].at[0, pl.ds(1, 2), 0],
            dst_ref=ghost_e.at[turn, run],
            send_sem=e_send.at[turn, run],
            recv_sem=e_recv.at[turn, run],
            device_id={"slab": left},
            device_id_type=pl.DeviceIdType.MESH,
        )

    def send_p(run, turn):
        return pltpu.make_async_remote_copy(
            src_ref=partial.at[turn, run],
            dst_ref=ghost_p.at[turn, run],
            send_sem=p_send.at[turn, run],
            recv_sem=p_recv.at[turn, run],
            device_id={"slab": right},
            device_id_type=pl.DeviceIdType.MESH,
        )

    def make_partial(run, turn):
        elec_x, elec_y, elec_z = (state[run, comp, top] for comp in range(3))
        partial[turn, run, 0] = state[run, 4, top] - c * (next_z(elec_x) - elec_x + elec_z)
        partial[turn, run, 1] = state[run, 5, top] + c * (elec_y + next_y(elec_x) - elec_x)

    def magnetic_x(run, row):
        elec_y, elec_z = state[run, 1, row], state[run, 2, row]
        state[run, 3, row] = state[run, 3, row] - c * (
            next_y(elec_z) - elec_z - (next_z(elec_y) - elec_y)
        )

    def magnetic_row(run, row):
        magnetic_x(run, row)
        elec_x, elec_y, elec_z = (state[run, comp, row] for comp in range(3))
        state[run, 4, row] = state[run, 4, row] - c * (
            next_z(elec_x) - elec_x - (state[run, 2, row + 1] - elec_z)
        )
        state[run, 5, row] = state[run, 5, row] - c * (
            state[run, 1, row + 1] - elec_y - (next_y(elec_x) - elec_x)
        )

    def keep(row, turn, elec_x, elec_y, elec_z):
        total = elec_x * state[0, 0, row] + elec_y * state[0, 1, row] + elec_z * state[0, 2, row]
        folded = total[0:8] + total[8:16] + total[16:24]
        if turn == STEPS - 1 and isinstance(row, int):
            late[row // top] = jnp.sum(folded, axis=0)
        elif turn == 0:
            acc[row] = folded
        else:
            acc[row] = acc[row] + folded

    def electric_row(run, row, turn, prior_hy, prior_hz):
        magn_x, magn_y, magn_z = (state[run, comp, row] for comp in range(3, 6))
        scaled = c * inverse[row]
        source = sources[run] * waves[run, :, turn : turn + 1]
        elec_x = (
            state[run, 0, row]
            + scaled * (magn_z - prior_y(magn_z) - (magn_y - prior_z(magn_y)))
            + source
        )
        elec_y = state[run, 1, row] + scaled * (magn_x - prior_z(magn_x) - (magn_z - prior_hz))
        elec_z = state[run, 2, row] + scaled * (magn_y - prior_hy - (magn_x - prior_y(magn_x)))
        state[run, 0, row] = elec_x
        state[run, 1, row] = elec_y
        state[run, 2, row] = elec_z
        if run == 1:
            keep(row, turn, elec_x, elec_y, elec_z)

    def interior(run, turn):
        magnetic_row(run, 0)

        @pl.loop(1, top)
        def _(row):
            magnetic_row(run, row)
            electric_row(run, row, turn, state[run, 4, row - 1], state[run, 5, row - 1])

        magnetic_x(run, top)
        ready(run, turn)

    def ready(run, turn):
        magn_x, magn_y, magn_z = (state[run, comp, 0] for comp in range(3, 6))
        scaled = c * inverse[0]
        reached = jnp.where(is_first, 0.0, scaled)
        source = sources[run] * waves[run, :, turn : turn + 1]
        elec_y, elec_z = state[run, 1, 0], state[run, 2, 0]
        soon[run, 5] = (
            state[run, 0, 0]
            + scaled * (magn_z - prior_y(magn_z) - (magn_y - prior_z(magn_y)))
            + source
        )
        soon[run, 0] = (
            elec_y + scaled * (magn_x - prior_z(magn_x) - magn_z) - reached * (c * elec_y)
        )
        soon[run, 1] = (
            elec_z + scaled * (magn_y - (magn_x - prior_y(magn_x))) - reached * (c * elec_z)
        )
        magn_x = state[run, 3, top]
        scaled = c * inverse[top]
        soon[run, 2] = state[run, 0, top] + source
        soon[run, 3] = state[run, 1, top] + scaled * (
            magn_x - prior_z(magn_x) + state[run, 5, top - 1]
        )
        soon[run, 4] = state[run, 2, top] - scaled * (
            magn_x - prior_y(magn_x) + state[run, 4, top - 1]
        )

    def boundary(run, turn):
        send_p(run, turn).wait_recv()
        reached = jnp.where(is_first, 0.0, c * inverse[0])
        elec_y = soon[run, 0] + reached * ghost_p[turn, run, 1]
        elec_z = soon[run, 1] - reached * ghost_p[turn, run, 0]
        if turn < STEPS - 1:
            edge[turn, run, 0] = elec_y
            edge[turn, run, 1] = elec_z
            send_e(run, turn + 1).start()
        else:
            state[run, 1, 0] = elec_y
            state[run, 2, 0] = elec_z
        send_e(run, turn).wait_recv()
        state[run, 0, 0] = soon[run, 5]
        if turn < STEPS - 1:
            state[run, 1, 0] = elec_y
            state[run, 2, 0] = elec_z
        scaled = c * inverse[top]
        magn_y = partial[turn, run, 0] + c * jnp.where(is_last, 0.0, ghost_e[turn, run, 1])
        magn_z = partial[turn, run, 1] - c * jnp.where(is_last, 0.0, ghost_e[turn, run, 0])
        elec_x = soon[run, 2] + scaled * (
            magn_z - prior_y(magn_z) - (magn_y - prior_z(magn_y))
        )
        elec_y = soon[run, 3] - scaled * magn_z
        elec_z = soon[run, 4] + scaled * magn_y
        if turn < STEPS - 1:
            partial[turn + 1, run, 0] = magn_y - c * (next_z(elec_x) - elec_x + elec_z)
            partial[turn + 1, run, 1] = magn_z + c * (elec_y + next_y(elec_x) - elec_x)
            send_p(run, turn + 1).start()
        state[run, 4, top] = magn_y
        state[run, 5, top] = magn_z
        state[run, 0, top] = elec_x
        state[run, 1, top] = elec_y
        state[run, 2, top] = elec_z
        if run == 1:
            for row in (0, top):
                keep(row, turn, *(state[1, comp, row] for comp in range(3)))

    def send_beside(side):
        return pltpu.make_async_remote_copy(
            src_ref=finish.at[pl.ds(0, 2)],
            dst_ref=beside.at[side],
            send_sem=beside_send.at[side],
            recv_sem=beside_recv.at[side],
            device_id={"slab": (right, left)[side]},
            device_id_type=pl.DeviceIdType.MESH,
        )

    def send_tile(partner):
        there = device(**partner)
        return pltpu.make_async_remote_copy(
            src_ref=outgoing.at[pl.ds(there["slab"], 1)],
            dst_ref=incoming.at[pl.ds(at_far * count + me, 1)],
            send_sem=tile_send,
            recv_sem=tile_recv,
            device_id=there,
            device_id_type=pl.DeviceIdType.MESH,
        )

    def hops(by):
        far_x, far_z = min(by["by_x"], SIDE_X - by["by_x"]), min(by["by_z"], SIDE_Z - by["by_z"])
        return far_x + far_z + (1 if by["by_y"] else 2 * by["by_far"])

    spokes = sorted(
        (
            dict(by_x=x, by_z=z, by_y=y, by_far=far)
            for x in range(SIDE_X)
            for z in range(SIDE_Z)
            for y in range(SIDE_Y)
            for far in range(2)
            if x + z + y + far
        ),
        key=hops,
        reverse=True,
    )

    def swap_cores(source, target):
        return pltpu.make_async_remote_copy(
            src_ref=source,
            dst_ref=target,
            send_sem=pair_send,
            recv_sem=pair_recv,
            device_id=device(by_core=1),
            device_id_type=pl.DeviceIdType.MESH,
        )

    pair = swap_cores(pairs.at[at_core], pairs.at[at_core])

    edges[0].wait()
    make_partial(0, 0)
    pl.semaphore_wait(barrier, 2 + len(greetings))
    send_e(0, 0).start()
    send_p(0, 0).start()
    edges[1].wait()
    make_partial(1, 0)
    send_e(1, 0).start()
    send_p(1, 0).start()
    greet(0)
    for copy in smalls:
        copy.wait()
    for run in range(2):
        level = lax.broadcasted_iota(jnp.int32, sources.shape[1:], 0)
        hit = level == planes[run]
        sources[run] = jnp.where(hit, jnp.broadcast_to(profiles[run], hit.shape), 0.0)

    width = density_hbm.shape[1]
    scale = step_size / math.sqrt(3 * STEPS * NZ * FREQS)
    tile_x = width // radius.shape[1]
    column = lax.broadcasted_iota(jnp.int32, (8, width), 1)
    line = lax.broadcasted_iota(jnp.int32, (8, width), 0)

    def spread(table):
        wide = jnp.zeros((8, width), jnp.float32)
        for tile in range(table.shape[1]):
            value = jnp.broadcast_to(table[:, tile : tile + 1], (8, width)).astype(jnp.float32)
            wide = jnp.where(column // tile_x == tile, value, wide)
        return wide

    finish[1] = scale * spread(mask)
    reach = spread(radius)
    rim_inside = ((line < 4) & (me < count - 1)) | ((line >= 4) & (me > 0))

    def prepare_weights():
        counts = rings(jnp.ones((8, width), jnp.float32), jnp.where(rim_inside, 1.0, 0.0))
        total = jnp.zeros((8, width), jnp.float32)
        for key in counts:
            total = total + jnp.maximum(reach - math.sqrt(key), 0.0) * counts[key]
        for place, key in enumerate(sorted(counts)):
            weights[place] = jnp.maximum(reach - math.sqrt(key), 0.0) / total

    medium.wait()
    loads[0].wait()
    interior(0, 0)
    greeted(0)
    loads[1].wait()
    interior(1, 0)
    greeted(1)
    for turn in range(STEPS):
        for run in range(2):
            boundary(run, turn)
        for run in range(2):
            if turn < STEPS - 1:
                interior(run, turn + 1)
            greeted(2 + 2 * turn + run)
        if turn == STEPS - 2:
            send_beside(0).start()
            send_beside(1).start()
            prepare_weights()
            local[...] = jnp.sum(acc[...], axis=1)

    ends = late[...]
    whole = local[...] + jnp.where(line == 0, ends[0:1], 0.0)
    pairs[at_core] = whole + jnp.where(line == top, ends[1:2], 0.0)
    pair.start()
    for side in range(2):
        send_beside(side).wait_recv()
    for place in range(2):
        rim = jnp.where(line < 4, beside[1, place], beside[0, place])
        finish[2 + place] = jnp.where(rim_inside, rim, 0.0)
    pair.wait_recv()
    whole = pairs[0] + pairs[1]
    sub = lax.broadcasted_iota(jnp.int32, (8, 128), 0)
    lane = lax.broadcasted_iota(jnp.int32, (8, 128), 1)
    strips = []
    for block in range(width // 128):
        v = whole[:, 128 * block : 128 * (block + 1)]
        for bit in range(3):
            v = swap_bits(v, bit, bit)
        for bit in range(3):
            v = swap_bits(v, bit, 3 + bit)
        strips += [v, pltpu.roll(v, 64, 1)]
    pieces = len(strips)
    for index in range(pieces):
        mine, above, below = strips[index], strips[(index + 1) % pieces], strips[index - 1]
        upper = pltpu.roll(jnp.where(sub == 0, above, mine), 7, 0)
        lower = pltpu.roll(jnp.where(sub == 7, below, mine), 1, 0)
        rim = jnp.where(lane < 32, upper, lower)
        packed = jnp.where(lane < 64, mine, pltpu.roll(rim, 64, 1))
        outgoing[8 * index : 8 * index + 8] = packed

    for spoke in spokes:
        send_tile(spoke).start()
    incoming[pl.ds(at_far * count + me, 1)] = outgoing[pl.ds(me, 1)]
    everyone = incoming.at[pl.ds(0, len(spokes))]
    pltpu.make_async_copy(everyone, everyone, tile_recv).wait()
    for turn in range(STEPS):
        for run in range(2):
            send_e(run, turn).wait_send()
            send_p(run, turn).wait_send()
    for side in range(2):
        send_beside(side).wait_send()
    pair.wait_send()
    pltpu.make_async_copy(everyone, everyone, tile_send).wait()


def write_kernel(
    state, incoming, finish, weights, forward_out, adjoint_out, projected_out, projected, sems
):
    copies = [
        pltpu.make_async_copy(state.at[run, comp], out.at[0, comp], sems.at[6 * run + comp])
        for run, out in enumerate((forward_out, adjoint_out))
        for comp in range(6)
    ]
    for copy in copies:
        copy.start()

    @pl.when(lax.axis_index("slab") >= 0)
    def _():
        lane = lax.broadcasted_iota(jnp.int32, (8, 128), 1)
        own_parts, rim_parts = [], []
        count = incoming.shape[0] // 2
        for index in range(0, count // 8, 2):
            halves = []
            for half in (index, index + 1):
                v = incoming[8 * half : 8 * half + 8] + incoming[count + 8 * half : count + 8 * half + 8]
                for bit in range(3):
                    v = swap_bits(v, bit, 3 + bit)
                halves.append(v)
            own_parts.append(jnp.where(lane < 64, halves[0], pltpu.roll(halves[1], 64, 1)))
            rim_parts.append(jnp.where(lane < 64, pltpu.roll(halves[0], 64, 1), halves[1]))
        own = finish[0] + finish[1] * jnp.concatenate(own_parts, axis=1)
        rim = finish[2] + finish[3] * jnp.concatenate(rim_parts, axis=1)
        sums = rings(own, rim)
        filtered = jnp.zeros_like(own)
        for place, key in enumerate(sorted(sums)):
            filtered = filtered + weights[place] * sums[key]
        base = math.tanh(sharpness * midpoint)
        projected[...] = (base + jnp.tanh(sharpness * (filtered - midpoint))) / (
            base + math.tanh(sharpness * (1.0 - midpoint))
        )

    copies.append(pltpu.make_async_copy(projected, projected_out, sems.at[12]))
    copies[-1].start()
    for copy in copies:
        copy.wait()


def yee(*operands):
    forward = operands[1]
    density = operands[10]
    rows, high, wide = forward.shape[2:]
    plane = (rows, high, wide)
    width = density.shape[1]
    count = lax.axis_size("slab")
    groups = lax.axis_size("freq")
    operands = [
        operand if place == 7 else pltpu.with_memory_space_constraint(operand, pltpu.HBM)
        for place, operand in enumerate(operands)
    ]
    results = pl.pallas_call(
        yee_kernel,
        out_shape=(
            pltpu.VMEM((2, 6) + plane, jnp.float32),
            pltpu.VMEM((2 * count, 128), jnp.float32),
            pltpu.VMEM((4, 8, width), jnp.float32),
            pltpu.VMEM((15, 8, width), jnp.float32),
        ),
        in_specs=[pl.BlockSpec(memory_space=pl.ANY)] * 11,
        out_specs=[pl.BlockSpec(memory_space=pltpu.VMEM)] * 4,
        scratch_shapes=[
            pltpu.VMEM(plane, jnp.float32),
            pltpu.VMEM((2, 1, STEPS), jnp.float32),
            pltpu.VMEM((2, 1, wide), jnp.float32),
            pltpu.SMEM((2,), jnp.int32),
            pltpu.VMEM((2, high, wide), jnp.float32),
            pltpu.VMEM((STEPS, 2, 2, high, wide), jnp.float32),
            pltpu.VMEM((STEPS, 2, 2, high, wide), jnp.float32),
            pltpu.VMEM((STEPS, 2, 2, high, wide), jnp.float32),
            pltpu.VMEM((STEPS - 1, 2, 2, high, wide), jnp.float32),
            pltpu.VMEM((2, 6, high, wide), jnp.float32),
            pltpu.VMEM((rows, 8, wide), jnp.float32),
            pltpu.VMEM(operands[8].shape, jnp.int32),
            pltpu.VMEM(operands[9].shape, jnp.int32),
            pltpu.VMEM((2, 2, 8, width), jnp.float32),
            pltpu.VMEM((2, rows, wide), jnp.float32),
            pltpu.VMEM((rows, wide), jnp.float32),
            pltpu.VMEM((2, wide), jnp.float32),
            pltpu.VMEM((count, 128), jnp.float32),
            pltpu.SemaphoreType.DMA((5,)),
            pltpu.SemaphoreType.DMA((9,)),
            pltpu.SemaphoreType.DMA((STEPS, 2)),
            pltpu.SemaphoreType.DMA((STEPS, 2)),
            pltpu.SemaphoreType.DMA((STEPS, 2)),
            pltpu.SemaphoreType.DMA((STEPS, 2)),
            pltpu.SemaphoreType.REGULAR((4,)),
            pltpu.SemaphoreType.DMA((2,)),
            pltpu.SemaphoreType.DMA((2,)),
            pltpu.SemaphoreType.DMA,
            pltpu.SemaphoreType.DMA,
            pltpu.SemaphoreType.DMA,
            pltpu.SemaphoreType.DMA,
        ],
        compiler_params=pltpu.CompilerParams(
            collective_id=0, has_side_effects=True, vmem_limit_bytes=40 << 20
        ),
        name="yee",
    )(*operands)
    results = [pltpu.with_memory_space_constraint(result, pltpu.VMEM) for result in results]
    return pl.pallas_call(
        write_kernel,
        out_shape=(
            jax.ShapeDtypeStruct(forward.shape, jnp.float32),
            jax.ShapeDtypeStruct(forward.shape, jnp.float32),
            jax.ShapeDtypeStruct(density.shape, jnp.float32),
        ),
        in_specs=[pl.BlockSpec(memory_space=pltpu.VMEM)] * 4,
        out_specs=[pl.BlockSpec(memory_space=pl.ANY)] * 3,
        scratch_shapes=[pltpu.VMEM(density.shape, jnp.float32), pltpu.SemaphoreType.DMA((13,))],
        compiler_params=pltpu.CompilerParams(vmem_limit_bytes=8 << 20),
        name="write",
    )(*results)


def on_device(
    inverse_permittivity,
    forward_fields,
    adjoint_fields,
    source_wave,
    source_profile,
    adjoint_wave,
    adjoint_profile,
    source_plane,
    monitor_plane,
    radius_map,
    design_mask,
    design_density,
):
    return yee(
        inverse_permittivity,
        forward_fields,
        adjoint_fields,
        source_wave,
        source_profile,
        adjoint_wave,
        adjoint_profile,
        jnp.concatenate([source_plane, monitor_plane]),
        radius_map,
        design_mask,
        design_density,
    )


def solution(mesh):
    return jax.shard_map(
        on_device,
        mesh=mesh,
        in_specs=(
            P("slab", None, None),
            P("freq", None, "slab", None, None),
            P("freq", None, "slab", None, None),
            P("freq", None),
            P("freq", None),
            P("freq", None),
            P("freq", None),
            P("freq"),
            P("freq"),
            P("slab", None),
            P("slab", None),
            P("slab", None),
        ),
        out_specs=(
            P("freq", None, "slab", None, None),
            P("freq", None, "slab", None, None),
            P("slab", None),
        ),
        check_vma=False,
    )
```
